128 devices in a mesh: member: 16 (over x_lo, y, core), lon: 8 (over x_hi, z).
Axes of the slice: x: 4 (x_hi: 2, x_lo: 2; x = x_hi * 2 + x_lo), y: 4, z: 4, core: 2. Of those that a mesh axis runs over, the one named last changes fastest.
Arguments:
- atmos: bfloat16 [16, 96, 96, 1024], P('member', None, None, 'lon'), may hold values from -6 to 6
- ocean: bfloat16 [96, 96, 1024], P(None, None, 'lon'), may hold values from -6 to 6
- land_mask: int32 [96, 1024], P(None, 'lon'), may hold values 0 or 1
- ice_mask: int32 [96, 1024], P(None, 'lon'), may hold values 0 or 1
- atm_kernel: float32 [2, 7, 7, 96], replicated, may hold values from -0.875 to 0.875
- atm_gain: float32 [2, 96], replicated, may hold values from 0.25 to 1.75
- atm_up: bfloat16 [2, 96, 384], replicated, may hold values from -0.625 to 0.625
- atm_down: bfloat16 [2, 384, 96], replicated, may hold values from -0.3125 to 0.3125
- atm_scale: float32 [2, 96], replicated, may hold values from 0.5 to 1.5
- flux_weight: bfloat16 [96, 32], replicated, may hold values from -0.625 to 0.625
- flux_lift: bfloat16 [2, 32, 96], replicated, may hold values from -1 to 1
- ocn_kernel: float32 [7, 7, 96], replicated, may hold values from -0.875 to 0.875
- ocn_gain: float32 [96], replicated, may hold values from 0.25 to 1.75
- ocn_up: bfloat16 [96, 384], replicated, may hold values from -0.625 to 0.625
- ocn_down: bfloat16 [384, 96], replicated, may hold values from -0.3125 to 0.3125
- ocn_scale: float32 [96], replicated, may hold values from 0.5 to 1.5
- surf_weight: bfloat16 [96, 8], replicated, may hold values from -0.625 to 0.625
- back_weight: bfloat16 [8, 96], replicated, may hold values from -2 to 2
Outputs:
- atmos_out: bfloat16 [16, 96, 96, 1024], P('member', None, None, 'lon')
- ocean_new: bfloat16 [96, 96, 1024], P('member', None, 'lon')
The draws below stay inside these ranges and needn't reach their ends.
All inputs are finite; a program needn't handle non-finite values. No bound on the sum of `land_mask` or of `ice_mask` on one device may be relied on, other than what follows from the above.
Results may differ from the reference program's by a relative error of at most 0.017.
Values may be sent and summed in bfloat16 or wider, within the bound.
A program may use at most 64 MiB of HBM per device.

```python
import jax
import jax.numpy as jnp
from jax import lax

C = 96
HID = 384
FLUX = 32
SURF = 8
LAT = 96
MEMBERS = 16
NLON = 1024


def set_ends(values, rng, smallest, largest):
    index_at = [jax.random.randint(jax.random.fold_in(rng, axis), (), 0, length) for axis, length in enumerate(values.shape)]
    longest = values.shape.index(max(values.shape))
    neighbour = index_at[:longest] + [(index_at[longest] + 1) % values.shape[longest]] + index_at[longest + 1:]
    return values.at[tuple(index_at)].set(smallest).at[tuple(neighbour)].set(largest)


def block_scale(own_key, shape, shards, smallest, largest):
    def one(position, parts):
        draws = jax.random.uniform(jax.random.fold_in(jax.random.fold_in(own_key, 6), position), (parts,), jnp.float32, smallest / len(shards), largest / len(shards))
        return jnp.repeat(jnp.exp(draws), shape[position] // parts).reshape((-1,) + (1,) * (len(shape) - position - 1))

    factor_of = one(*shards[0])
    for cut in shards[1:]:
        factor_of = factor_of * one(*cut)
    return factor_of


def centred(own_key, extent, width, limit, shards=(), held_as=jnp.bfloat16):
    values = width * jax.random.normal(own_key, extent, jnp.float32)
    if shards:
        values = values * block_scale(own_key, extent, shards, -0.22, 0.18)
    return jnp.clip(values, -limit, limit).astype(held_as)


def setup_inputs(seed: int = 0) -> dict:
    keys = jax.random.split(jax.random.key(seed), 19)
    return {
        "atmos": centred(keys[0], (MEMBERS, LAT, C, NLON), 1.0, 6.0, ((0, 16), (3, 8))),
        "ocean": centred(keys[1], (LAT, C, NLON), 1.0, 6.0, ((2, 8),)),
        "land_mask": set_ends((jax.random.randint(keys[2], (LAT, NLON), 0, 10) < 3).astype(jnp.int32), jax.random.fold_in(keys[2], 1), 0, 1),
        "ice_mask": set_ends((jax.random.randint(keys[3], (LAT, NLON), 0, 4) < 1).astype(jnp.int32), jax.random.fold_in(keys[3], 1), 0, 1),
        "atm_kernel": centred(keys[4], (2, 7, 7, C), 49 ** -0.5, 0.875, (), jnp.float32),
        "atm_gain": jnp.clip(1.0 + 0.15 * jax.random.normal(keys[5], (2, C), jnp.float32), 0.25, 1.75),
        "atm_up": centred(keys[6], (2, C, HID), C ** -0.5, 0.625),
        "atm_down": centred(keys[7], (2, HID, C), HID ** -0.5, 0.3125),
        "atm_scale": jnp.clip(jax.random.uniform(keys[8], (2, C), jnp.float32, 0.5, 1.5), 0.5, 1.5),
        "flux_weight": centred(keys[9], (C, FLUX), C ** -0.5, 0.625),
        "flux_lift": centred(keys[10], (2, FLUX, C), FLUX ** -0.5, 1.0),
        "ocn_kernel": centred(keys[11], (7, 7, C), 49 ** -0.5, 0.875, (), jnp.float32),
        "ocn_gain": jnp.clip(1.0 + 0.15 * jax.random.normal(keys[12], (C,), jnp.float32), 0.25, 1.75),
        "ocn_up": centred(keys[13], (C, HID), C ** -0.5, 0.625),
        "ocn_down": centred(keys[14], (HID, C), HID ** -0.5, 0.3125),
        "ocn_scale": jnp.clip(jax.random.uniform(keys[15], (C,), jnp.float32, 0.5, 1.5), 0.5, 1.5),
        "surf_weight": centred(keys[16], (C, SURF), C ** -0.5, 0.625),
        "back_weight": centred(keys[17], (SURF, C), SURF ** -0.5, 2.0),
    }


def contract(form, left, right):
    return jnp.einsum(form, left.astype(jnp.float32), right.astype(jnp.float32))

def cycle_pad(field):
    padded = jnp.pad(field, ((3, 3), (0, 0), (0, 0)))
    return jnp.concatenate([padded[:, :, -3:], padded, padded[:, :, :3]], axis=2)

def mixer(field, padded, kernel, gain, up_proj, down_proj, scale, keep):
    rows = field.shape[0]
    cols = field.shape[2]
    acc = jnp.zeros(field.shape, jnp.float32)
    for i in range(7):
        for j in range(7):
            acc = acc + padded[i:i + rows, :, j:j + cols].astype(jnp.float32) * kernel[i, j][:, None]
    center = acc - lax.optimization_barrier(jnp.mean(acc, axis=1, keepdims=True))
    spread = lax.optimization_barrier(jnp.mean(center * center, axis=1, keepdims=True))
    normed = (center * lax.rsqrt(spread + 1e-06) * gain[:, None]).astype(jnp.bfloat16)
    hidden = jax.nn.gelu(contract('lcw,ch->lhw', normed, up_proj)).astype(jnp.bfloat16)
    branch = contract('lhw,hc->lcw', hidden, down_proj)
    result = field.astype(jnp.float32) + scale[:, None] * branch
    if keep is not None:
        result = result * keep[:, None, :]
    return result.astype(jnp.bfloat16)

def reference(atmos, ocean, land_mask, ice_mask, atm_kernel, atm_gain, atm_up, atm_down, atm_scale, flux_weight, flux_lift, ocn_kernel, ocn_gain, ocn_up, ocn_down, ocn_scale, surf_weight, back_weight):
    sea = (1 - land_mask).astype(jnp.float32)
    ice = ice_mask.astype(jnp.float32)

    def member_step(state):
        for layer in range(2):
            state = mixer(state, cycle_pad(state), atm_kernel[layer], atm_gain[layer], atm_up[layer], atm_down[layer], atm_scale[layer], None)
        flux = jax.nn.gelu(contract('lcw,cf->lfw', state, flux_weight))
        return (state, flux)
    blocks, fluxes = lax.map(member_step, atmos)
    flux_low = (lax.optimization_barrier(jnp.sum(fluxes, axis=0)) / MEMBERS).astype(jnp.bfloat16)
    open_term = contract('lfw,fc->lcw', flux_low, flux_lift[0])
    ice_term = contract('lfw,fc->lcw', flux_low, flux_lift[1])
    forcing = sea[:, None, :] * ((1.0 - ice)[:, None, :] * open_term + ice[:, None, :] * ice_term)
    ocean_mid = (ocean.astype(jnp.float32) + forcing).astype(jnp.bfloat16)
    ocean_new = mixer(ocean_mid, cycle_pad(ocean_mid), ocn_kernel, ocn_gain, ocn_up, ocn_down, ocn_scale, sea)
    surface = contract('lcw,cs->lsw', ocean_new, surf_weight).astype(jnp.bfloat16)
    coupling = sea[:, None, :] * contract('lsw,sc->lcw', surface, back_weight)

    def couple(state):
        return (state.astype(jnp.float32) + coupling).astype(jnp.bfloat16)
    atmos_out = lax.map(couple, blocks)
    return (atmos_out, ocean_new)
```

```python
import functools

import jax
import jax.numpy as jnp
from jax import lax
from jax.experimental import pallas as pl
from jax.experimental.pallas import tpu as pltpu
from jax.sharding import PartitionSpec as P

BF16 = jnp.bfloat16
F32 = jnp.float32
MESH = pl.DeviceIdType.MESH

C = 96
W = 128
LAT = 96
GROUP = 16
GROUPS = C // GROUP
OUT = 10
WIN = 16
PAIR = 2 * OUT
TILES = 5
SLOT = 6
TAPS = 7
DEPTH = TAPS * WIN * GROUP
ROWS_IN = 106
TANH_A = 2.0 * 0.7978845608028654
TANH_B = 8.0 * 0.7978845608028654 * 0.044715


def half_gelu(half):
    return half + half * jnp.tanh(half * (TANH_A + TANH_B * (half * half)))


def half_gelu_low(half):
    half = half.astype(BF16)
    return half + half * jnp.tanh(half * (BF16(TANH_A) + BF16(TANH_B) * (half * half)))


def lanes(shape):
    return lax.broadcasted_iota(jnp.int32, shape, len(shape) - 1)


def turn(v, shift):
    shift = shift % W
    return v if shift == 0 else pltpu.roll(v, shift, 1)


def band_matrix(kernel_of, taps, bands, outs):
    taps[...] = jnp.zeros(taps.shape, F32)
    for i in range(TAPS):
        taps[8 * i : 8 * i + TAPS, 0:C] = kernel_of(i)
    by_channel = jnp.transpose(taps[...])[0:C].astype(BF16)
    row = lax.broadcasted_iota(jnp.int32, (W, DEPTH), 0)
    lane = lanes((W, DEPTH))
    spread = (row % 8 == lane // (WIN * GROUP)) & (row // 8 == (lane % (WIN * GROUP)) // GROUP)
    wide = jnp.dot(by_channel, spread.astype(F32).astype(BF16), preferred_element_type=F32)
    crow = lax.broadcasted_iota(jnp.int32, (C, DEPTH), 0)
    wide = jnp.where(crow % GROUP == lanes((C, DEPTH)) % GROUP, wide, 0.0).astype(BF16)
    for g in range(GROUPS):
        base = wide[GROUP * g : GROUP * g + GROUP]
        for l in range(outs):
            bands[g, GROUP * l : GROUP * l + GROUP, :] = (
                base if l == 0 else pltpu.roll(base, GROUP * l, 1)
            )


def columns(vector_row):
    return jnp.transpose(jnp.broadcast_to(vector_row, (W, C)))


def shifted(cells, edge, d):
    if d == 0:
        return cells
    lane = lanes(cells.shape)
    if d > 0:
        return pltpu.roll(jnp.where(lane < d, edge, cells), W - d, 1)
    return pltpu.roll(jnp.where(lane >= W + d, edge, cells), -d, 1)


def conv_part(cells, edges, g, row):
    part = cells[pl.ds(row, WIN), GROUP * g : GROUP * g + GROUP, :].reshape(WIN * GROUP, W)
    edge = edges[pl.ds(row, WIN), GROUP * g : GROUP * g + GROUP, :].reshape(WIN * GROUP, W)
    return jnp.concatenate([shifted(part, edge, j - 3) for j in range(TAPS)], 0)


def conv_pair(cells, edges, bands, acc, row):
    for g in range(GROUPS):
        right = jnp.concatenate(
            [conv_part(cells, edges, g, row), conv_part(cells, edges, g, row + OUT)], 1
        )
        out = jnp.dot(bands[g], right, preferred_element_type=F32)
        for half in range(2):
            acc[OUT * half : OUT * half + OUT, GROUP * g : GROUP * g + GROUP, :] = out[
                :, half * W : half * W + W
            ].reshape(OUT, GROUP, W)


def normed(a, gain):
    center = a - jnp.mean(a, axis=0, keepdims=True)
    spread = jnp.mean(center * center, axis=0, keepdims=True)
    return (center * lax.rsqrt(spread + 1e-6) * gain).astype(BF16)


def branch(acc, count, up, down, gain):
    n = jnp.concatenate([normed(acc[k], gain) for k in range(count)], 1)
    hidden = half_gelu_low(jnp.dot(up, n, preferred_element_type=F32))
    return jnp.dot(down, hidden, preferred_element_type=F32)


def pack_edges(row_of, count):
    lane = lanes((C, W))
    slot = jnp.where(lane >= W - 3, 0, (lane + 3) // SLOT)
    packed = row_of(0)
    for k in range(1, count):
        packed = jnp.where(slot == k, turn(row_of(k), SLOT * k), packed)
    return packed


def joined_edges(from_left, from_right):
    lane = lanes((C, W))
    left_side = (lane >= W - 3) | ((lane < W - 5) & ((lane + 3) % SLOT < 3))
    return jnp.where(left_side, from_left, from_right)


def coupled_kernel(
    x_hbm, ocean_hbm, land, icem, ak, ag, au, ad, asc, fw, fl, okn, og, ou, od, osc, sw,
    y_hbm, surf_out, ocean_out,
    xp, xe, yp, ye, y2, bands1, bands2, bands3, acc, taps, up_t, down_t, gains, scales,
    ups_o, fw_t, fl_t, sw_t,
    pack1, fl1, fr1, pack2, fl2, fr2, flux, fluxes, oc, mid, mide, opack, orow_lo, orow_hi, oedge,
    surf, surfs,
    in_sem, oc_sem, out_sem, s1, r1, s2, r2, fs, fr, os_, or_, ss, sr, o_sem,
):
    m = lax.axis_index("member")
    b = lax.axis_index("lon")
    members = 16
    bands = 8
    right = lax.rem(b + 1, bands)
    left = lax.rem(b + bands - 1, bands)
    above = lax.rem(m + members - 1, members)
    below = lax.rem(m + 1, members)

    barrier = pltpu.get_barrier_semaphore()
    for side in (left, right):
        for who in (above, m, below):
            pl.semaphore_signal(barrier, inc=1, device_id=(who, side), device_id_type=MESH)

    @pl.loop(1, members)
    def _(k):
        pl.semaphore_signal(
            barrier, inc=1, device_id=(lax.rem(m + k, members), b), device_id_type=MESH
        )

    def load(p, rows):
        return pltpu.make_async_copy(
            x_hbm.at[0, pl.ds(p * PAIR, rows)], xp.at[pl.ds(3 + p * PAIR, rows)], in_sem.at[p]
        )

    for p in range(TILES):
        load(p, min(PAIR, LAT - p * PAIR)).start()
    oc_copy = pltpu.make_async_copy(ocean_hbm.at[pl.ds(6 * m, 6)], oc, oc_sem)
    oc_copy.start()

    for ref in (xp, xe, yp, ye):
        ref[0:3] = jnp.zeros((3, C, W), BF16)
        ref[99:ROWS_IN] = jnp.zeros((ROWS_IN - 99, C, W), BF16)

    def sends(p, packed, from_left, from_right, ssem, rsem):
        return (
            pltpu.make_async_remote_copy(
                packed.at[p], from_left.at[p], ssem.at[0, p], rsem.at[0, p],
                device_id=(m, right), device_id_type=MESH,
            ),
            pltpu.make_async_remote_copy(
                packed.at[p], from_right.at[p], ssem.at[1, p], rsem.at[1, p],
                device_id=(m, left), device_id_type=MESH,
            ),
        )

    for p in range(TILES):
        load(p, min(PAIR, LAT - p * PAIR)).wait()
        pack1[p] = pack_edges(lambda k: xp[3 + p * PAIR + k], min(PAIR, LAT - p * PAIR))

    pl.semaphore_wait(barrier, members - 1 + 6)

    for p in range(TILES):
        for copy in sends(p, pack1, fl1, fr1, s1, r1):
            copy.start()

    band_matrix(lambda i: ak[0, i], taps, bands1, OUT)
    band_matrix(lambda i: ak[1, i], taps, bands2, OUT)
    band_matrix(lambda i: okn[i], taps, bands3, 6)
    for layer in range(2):
        up_t[layer] = (jnp.transpose(au[layer].astype(F32)) * 0.5).astype(BF16)
        down_t[layer] = jnp.transpose(ad[layer].astype(F32)).astype(BF16)
        gains[layer] = columns(ag[layer : layer + 1])
        scales[layer] = columns(asc[layer : layer + 1])
    up_t[2] = (jnp.transpose(ou[...].astype(F32)) * 0.5).astype(BF16)
    down_t[2] = jnp.transpose(od[...].astype(F32)).astype(BF16)
    gains[2] = columns(og[...])
    scales[2] = columns(osc[...])
    fw_t[...] = (jnp.transpose(fw[...].astype(F32)) * 0.5).astype(BF16)
    for s in range(2):
        fl_t[s] = jnp.transpose(fl[s].astype(F32)).astype(BF16)
    sw_t[...] = jnp.transpose(sw[...].astype(F32)).astype(BF16)

    def spread_edges(p, from_left, from_right, edges):
        both = joined_edges(from_left[p], from_right[p])
        for k in range(PAIR):
            edges[3 + p * PAIR + k] = turn(both, -SLOT * k)

    def arrive(p, packed, from_left, from_right, ssem, rsem, edges):
        for copy in sends(p, packed, from_left, from_right, ssem, rsem):
            copy.wait()
        spread_edges(p, from_left, from_right, edges)

        @pl.when(p == TILES - 1)
        def _():
            edges[99:ROWS_IN] = jnp.zeros((ROWS_IN - 99, C, W), BF16)

    arrive(0, pack1, fl1, fr1, s1, r1, xe)

    @pl.loop(0, TILES)
    def _(p):
        @pl.when(p < TILES - 1)
        def _():
            arrive(p + 1, pack1, fl1, fr1, s1, r1, xe)

        conv_pair(xp, xe, bands1, acc, p * PAIR)
        add = branch(acc, PAIR, up_t[0], down_t[0], gains[0])
        for k in range(PAIR):
            yp[3 + p * PAIR + k] = (
                xp[3 + p * PAIR + k].astype(F32) + scales[0] * add[:, k * W : k * W + W]
            ).astype(BF16)
        pack2[p] = pack_edges(lambda k: yp[3 + p * PAIR + k], PAIR)
        for copy in sends(p, pack2, fl2, fr2, s2, r2):
            copy.start()

    yp[99:ROWS_IN] = jnp.zeros((ROWS_IN - 99, C, W), BF16)

    def flux_copy(d):
        return pltpu.make_async_remote_copy(
            flux.at[pl.ds(6 * d, 6)], fluxes.at[m], fs.at[d], fr.at[m],
            device_id=(d, b), device_id_type=MESH,
        )

    def flux_arrival(k):
        return pltpu.make_async_remote_copy(
            flux.at[pl.ds(6 * k, 6)], fluxes.at[k], fs.at[k], fr.at[k],
            device_id=(k, b), device_id_type=MESH,
        )

    def store(p, rows):
        return pltpu.make_async_copy(
            y2.at[pl.ds(p * PAIR, rows)], y_hbm.at[pl.ds(p * PAIR, rows)], out_sem.at[p]
        )

    arrive(0, pack2, fl2, fr2, s2, r2, ye)

    @pl.loop(0, TILES)
    def _(p):
        @pl.when(p < TILES - 1)
        def _():
            arrive(p + 1, pack2, fl2, fr2, s2, r2, ye)

        conv_pair(yp, ye, bands2, acc, p * PAIR)
        add = branch(acc, PAIR, up_t[1], down_t[1], gains[1])
        rows = []
        for k in range(PAIR):
            rows.append(
                (
                    yp[3 + p * PAIR + k].astype(F32) + scales[1] * add[:, k * W : k * W + W]
                ).astype(BF16)
            )
            y2[p * PAIR + k] = rows[k]
        out = half_gelu(
            jnp.dot(fw_t[...], jnp.concatenate(rows, 1), preferred_element_type=F32)
        ).astype(BF16)
        for k in range(PAIR):
            flux[p * PAIR + k] = out[:, k * W : k * W + W]

        @pl.when(p < TILES - 1)
        def _():
            store(p, PAIR).start()

        @pl.when(p == TILES - 1)
        def _():
            store(p, LAT - PAIR * (TILES - 1)).start()

        last = jnp.minimum((PAIR * (p + 1)) // 6, members)

        @pl.loop((PAIR * p) // 6, last)
        def _(d):
            @pl.when(d != m)
            def _():
                flux_copy(d).start()

    fluxes[m] = flux[pl.ds(6 * m, 6)]

    @pl.loop(0, members)
    def _(k):
        @pl.when(k != m)
        def _():
            flux_arrival(k).wait_recv()

    total = fluxes[0].astype(F32)
    for k in range(1, members):
        total = total + fluxes[k].astype(F32)
    low = (total * (1.0 / members)).astype(BF16)
    low = jnp.concatenate([low[k] for k in range(6)], 1)
    open_term = jnp.dot(fl_t[0], low, preferred_element_type=F32)
    ice_term = jnp.dot(fl_t[1], low, preferred_element_type=F32)
    oc_copy.wait()
    mid[...] = jnp.zeros(mid.shape, BF16)
    mide[...] = jnp.zeros(mide.shape, BF16)
    for k in range(6):
        sea = (1 - land[pl.ds(6 * m + k, 1), :]).astype(F32)
        ice = icem[pl.ds(6 * m + k, 1), :].astype(F32)
        at = slice(k * W, k * W + W)
        forcing = sea * ((1.0 - ice) * open_term[:, at] + ice * ice_term[:, at])
        mid[3 + k] = (oc[k].astype(F32) + forcing).astype(BF16)
    opack[...] = pack_edges(lambda k: mid[3 + k], 6)

    def ocean_rows_up():
        return pltpu.make_async_remote_copy(
            mid.at[pl.ds(3, 3)], orow_hi, os_.at[0], or_.at[0],
            device_id=(above, b), device_id_type=MESH,
        )

    def ocean_rows_down():
        return pltpu.make_async_remote_copy(
            mid.at[pl.ds(6, 3)], orow_lo, os_.at[1], or_.at[1],
            device_id=(below, b), device_id_type=MESH,
        )

    def edge_copy(step, side):
        who = (above, m, below)[step + 1]
        return pltpu.make_async_remote_copy(
            opack, oedge.at[1 - step, side], os_.at[2 + 2 * (step + 1) + side],
            or_.at[2 + 2 * (1 - step) + side],
            device_id=(who, (right, left)[side]), device_id_type=MESH,
        )

    has_above = m > 0
    has_below = m < members - 1

    def guarded(flag, act):
        if flag is None:
            act()
        else:
            pl.when(flag)(act)

    guards = {-1: has_above, 0: None, 1: has_below}
    pl.when(has_above)(lambda: ocean_rows_up().start())
    pl.when(has_below)(lambda: ocean_rows_down().start())
    for step in (0, -1, 1):
        for side in range(2):
            guarded(guards[step], lambda: edge_copy(step, side).start())

    pl.when(has_below)(lambda: ocean_rows_up().wait_recv())
    pl.when(has_above)(lambda: ocean_rows_down().wait_recv())
    for step in (0, 1, -1):
        for side in range(2):
            guarded(guards[-step], lambda: edge_copy(step, side).wait_recv())

    for step, first, count, at in ((-1, 3, 3, 0), (0, 0, 6, 3), (1, 0, 3, 9)):
        def fill(step=step, first=first, count=count, at=at):
            both = joined_edges(oedge[step + 1, 0], oedge[step + 1, 1])
            for k in range(count):
                mide[at + k] = turn(both, -SLOT * (first + k))

        guarded(guards[step], fill)

    pl.when(has_above)(lambda: ocean_rows_up().wait_send())
    pl.when(has_below)(lambda: ocean_rows_down().wait_send())
    for step in (0, -1, 1):
        for side in range(2):
            guarded(guards[step], lambda: edge_copy(step, side).wait_send())

    @pl.when(has_above)
    def _():
        mid[0:3] = orow_lo[...]

    @pl.when(has_below)
    def _():
        mid[9:12] = orow_hi[...]

    for g in range(GROUPS):
        out = jnp.dot(bands3[g], conv_part(mid, mide, g, 0), preferred_element_type=F32)
        acc[0:6, GROUP * g : GROUP * g + GROUP, :] = out.reshape(6, GROUP, W)
    add = branch(acc, 6, up_t[2], down_t[2], gains[2])
    rows = []
    for k in range(6):
        sea = (1 - land[pl.ds(6 * m + k, 1), :]).astype(F32)
        new = ((mid[3 + k].astype(F32) + scales[2] * add[:, k * W : k * W + W]) * sea).astype(BF16)
        ocean_out[k] = new
        rows.append(new)
    top = jnp.dot(sw_t[...], jnp.concatenate(rows, 1), preferred_element_type=F32).astype(BF16)
    for k in range(6):
        surf[k] = top[:, k * W : k * W + W]

    def surf_copy(d):
        return pltpu.make_async_remote_copy(
            surf, surfs.at[m], ss.at[d], sr.at[m], device_id=(d, b), device_id_type=MESH
        )

    def surf_arrival(k):
        return pltpu.make_async_remote_copy(
            surf, surfs.at[k], ss.at[k], sr.at[k], device_id=(k, b), device_id_type=MESH
        )

    @pl.loop(1, members)
    def _(k):
        surf_copy(lax.rem(m + k, members)).start()

    surfs[m] = surf[...]

    @pl.loop(1, members)
    def _(k):
        surf_arrival(lax.rem(m + k, members)).wait_recv()

    surf_out[...] = surfs[...]

    @pl.loop(1, members)
    def _(k):
        surf_copy(lax.rem(m + k, members)).wait_send()
        flux_copy(lax.rem(m + k, members)).wait_send()

    for p in range(TILES):
        store(p, min(PAIR, LAT - p * PAIR)).wait()


def couple_kernel(y, surf, land, back, out):
    back_t = jnp.transpose(back[...].astype(F32)).astype(BF16)
    rows = y.shape[0]
    top = jnp.concatenate([surf[k] for k in range(rows)], 1)
    add = jnp.dot(back_t, top, preferred_element_type=F32)
    for k in range(rows):
        sea = (1 - land[k : k + 1, :]).astype(F32)
        out[0, k] = (y[k].astype(F32) + sea * add[:, k * W : k * W + W]).astype(BF16)


def local(
    atmos, ocean, land_mask, ice_mask, atm_kernel, atm_gain, atm_up, atm_down, atm_scale,
    flux_weight, flux_lift, ocn_kernel, ocn_gain, ocn_up, ocn_down, ocn_scale,
    surf_weight, back_weight,
):
    vmem = pl.BlockSpec(memory_space=pltpu.VMEM)
    hbm = pl.BlockSpec(memory_space=pl.ANY)
    dma = pltpu.SemaphoreType.DMA
    V = pltpu.VMEM
    field = V((ROWS_IN, C, W), BF16)
    packed = V((TILES, C, W), BF16)
    y, surface, ocean_rows = pl.pallas_call(
        coupled_kernel,
        out_shape=(
            jax.ShapeDtypeStruct((LAT, C, W), BF16),
            jax.ShapeDtypeStruct((16, 6, 8, W), BF16),
            jax.ShapeDtypeStruct((6, C, W), BF16),
        ),
        in_specs=[hbm, hbm] + [vmem] * 15,
        out_specs=(hbm, vmem, vmem),
        scratch_shapes=[
            field, field, field, field, V((TILES * PAIR, C, W), BF16),
            V((GROUPS, GROUP * OUT, DEPTH), BF16), V((GROUPS, GROUP * OUT, DEPTH), BF16),
            V((GROUPS, GROUP * 6, DEPTH), BF16),
            V((PAIR, C, W), F32), V((W, W), F32),
            V((3, 384, C), BF16), V((3, C, 384), BF16), V((3, C, W), F32), V((3, C, W), F32),
            V((8, W), F32), V((32, C), BF16), V((2, C, 32), BF16), V((8, C), BF16),
            packed, packed, packed, packed, packed, packed,
            V((TILES * PAIR, 32, W), BF16), V((16, 6, 32, W), BF16),
            V((6, C, W), BF16), V((WIN, C, W), BF16), V((WIN, C, W), BF16), V((C, W), BF16),
            V((3, C, W), BF16), V((3, C, W), BF16), V((3, 2, C, W), BF16),
            V((6, 8, W), BF16), V((16, 6, 8, W), BF16),
            dma((TILES,)), dma, dma((TILES,)),
            dma((2, TILES)), dma((2, TILES)), dma((2, TILES)), dma((2, TILES)),
            dma((16,)), dma((16,)), dma((8,)), dma((8,)), dma((16,)), dma((16,)), dma,
        ],
        compiler_params=pltpu.CompilerParams(
            collective_id=0, has_side_effects=True, vmem_limit_bytes=60 * 2**20
        ),
        name="coupled",
    )(
        atmos, ocean, land_mask, ice_mask, atm_kernel, atm_gain, atm_up, atm_down, atm_scale,
        flux_weight, flux_lift, ocn_kernel, ocn_gain.reshape(1, C), ocn_up, ocn_down,
        ocn_scale.reshape(1, C), surf_weight,
    )
    step = 16
    atmos_out = pl.pallas_call(
        couple_kernel,
        grid=(LAT // step,),
        out_shape=jax.ShapeDtypeStruct((1, LAT, C, W), BF16),
        in_specs=[
            pl.BlockSpec((step, C, W), lambda t: (t, 0, 0)),
            pl.BlockSpec((step, 8, W), lambda t: (t, 0, 0)),
            pl.BlockSpec((step, W), lambda t: (t, 0)),
            pl.BlockSpec((8, C), lambda t: (0, 0)),
        ],
        out_specs=pl.BlockSpec((1, step, C, W), lambda t: (0, t, 0, 0)),
        name="couple",
    )(y, surface.reshape(LAT, 8, W), land_mask, back_weight)
    return (atmos_out, ocean_rows)


def solution(mesh):
    in_specs = (
        P("member", None, None, "lon"),
        P(None, None, "lon"),
        P(None, "lon"),
        P(None, "lon"),
    ) + (P(),) * 14
    out_specs = (P("member", None, None, "lon"), P("member", None, "lon"))
    return jax.shard_map(local, mesh=mesh, in_specs=in_specs, out_specs=out_specs, check_vma=False)
```

```python
import jax
import jax.numpy as jnp
from jax import lax
from jax.experimental import pallas as pl
from jax.experimental.pallas import tpu as pltpu
from jax.sharding import PartitionSpec as P

BF16 = jnp.bfloat16
F32 = jnp.float32
MESH = pl.DeviceIdType.MESH

C = 96
W = 128
LAT = 96
GROUP = 16
GROUPS = C // GROUP
OUT = 10
WIN = 16
PAIR = 2 * OUT
TILES = 5
SLOT = 6
TAPS = 7
DEPTH = TAPS * WIN * GROUP
ROWS_IN = 106
TANH_A = 2.0 * 0.7978845608028654
TANH_B = 8.0 * 0.7978845608028654 * 0.044715


def half_gelu(half):
    return half + half * jnp.tanh(half * (TANH_A + TANH_B * (half * half)))


def half_gelu_low(half):
    half = half.astype(BF16)
    return half + half * jnp.tanh(half * (BF16(TANH_A) + BF16(TANH_B) * (half * half)))


def lanes(shape):
    return lax.broadcasted_iota(jnp.int32, shape, len(shape) - 1)


def turn(v, shift):
    shift = shift % W
    return v if shift == 0 else pltpu.roll(v, shift, 1)


def band_matrix(kernel_of, taps, bands, outs):
    taps[...] = jnp.zeros(taps.shape, F32)
    for i in range(TAPS):
        taps[8 * i : 8 * i + TAPS, 0:C] = kernel_of(i)
    by_channel = jnp.transpose(taps[...])[0:C].astype(BF16)
    row = lax.broadcasted_iota(jnp.int32, (W, DEPTH), 0)
    lane = lanes((W, DEPTH))
    spread = (row % 8 == lane // (WIN * GROUP)) & (row // 8 == (lane % (WIN * GROUP)) // GROUP)
    wide = jnp.dot(by_channel, spread.astype(F32).astype(BF16), preferred_element_type=F32)
    crow = lax.broadcasted_iota(jnp.int32, (C, DEPTH), 0)
    wide = jnp.where(crow % GROUP == lanes((C, DEPTH)) % GROUP, wide, 0.0).astype(BF16)
    for g in range(GROUPS):
        base = wide[GROUP * g : GROUP * g + GROUP]
        for l in range(outs):
            bands[g, GROUP * l : GROUP * l + GROUP, :] = (
                base if l == 0 else pltpu.roll(base, GROUP * l, 1)
            )


def columns(vector_row):
    return jnp.transpose(jnp.broadcast_to(vector_row, (W, C)))


def shifted(cells, edge, d):
    if d == 0:
        return cells
    lane = lanes(cells.shape)
    if d > 0:
        return pltpu.roll(jnp.where(lane < d, edge, cells), W - d, 1)
    return pltpu.roll(jnp.where(lane >= W + d, edge, cells), -d, 1)


def conv_part(cells, edges, g, row):
    part = cells[pl.ds(row, WIN), GROUP * g : GROUP * g + GROUP, :].reshape(WIN * GROUP, W)
    edge = edges[pl.ds(row, WIN), GROUP * g : GROUP * g + GROUP, :].reshape(WIN * GROUP, W)
    return jnp.concatenate([shifted(part, edge, j - 3) for j in range(TAPS)], 0)


def conv_group(cells, edges, bands, acc, row, g):
    right = jnp.concatenate(
        [conv_part(cells, edges, g, row), conv_part(cells, edges, g, row + OUT)], 1
    )
    out = jnp.dot(bands[g], right, preferred_element_type=F32)
    for half in range(2):
        acc[OUT * half : OUT * half + OUT, GROUP * g : GROUP * g + GROUP, :] = out[
            :, half * W : half * W + W
        ].reshape(OUT, GROUP, W)


def normed(a, gain):
    center = a - jnp.mean(a, axis=0, keepdims=True)
    spread = jnp.mean(center * center, axis=0, keepdims=True)
    return (center * lax.rsqrt(spread + 1e-6) * gain).astype(BF16)


def branch(acc, first, count, up, down, gain):
    n = jnp.concatenate([normed(acc[first + k], gain) for k in range(count)], 1)
    hidden = half_gelu_low(jnp.dot(up, n, preferred_element_type=F32))
    return jnp.dot(down, hidden, preferred_element_type=F32)


def pack_edges(row_of, count):
    lane = lanes((C, W))
    slot = jnp.where(lane >= W - 3, 0, (lane + 3) // SLOT)
    packed = row_of(0)
    for k in range(1, count):
        packed = jnp.where(slot == k, turn(row_of(k), SLOT * k), packed)
    return packed


def pack_thin(row_of, count, shift):
    slot = lanes((C, W)) // 3
    packed = turn(row_of(0), shift)
    for k in range(1, count):
        packed = jnp.where(slot == k, turn(row_of(k), 3 * k + shift), packed)
    return packed


def joined_edges(from_left, from_right):
    lane = lanes((C, W))
    left_side = (lane >= W - 3) | ((lane < W - 5) & ((lane + 3) % SLOT < 3))
    return jnp.where(left_side, from_left, from_right)


def coupled_kernel(
    x_hbm, ocean_hbm, land, icem, ak, ag, au, ad, asc, fw, fl, okn, og, ou, od, osc, sw, bw,
    out_hbm, ocean_out,
    xp, xe, yp, ye, y2, bands1, bands2, bands3, acc0, acc1, taps, up_t, down_t, gains, scales,
    fw_t, fl_t, sw_t, bw_t,
    pack_r, pack_l, fl1, fr1, pack2, fl2, fr2, flux, fluxes, oc, mid, mide, opack, orow_lo, orow_hi,
    oedge, surf, surfs,
    in_sem, oc_sem, out_sem, s1, r1, s2, r2, fs, fr, os_, or_, ss, sr,
):
    m = lax.axis_index("member")
    b = lax.axis_index("lon")
    members = 16
    bands = 8
    right = lax.rem(b + 1, bands)
    left = lax.rem(b + bands - 1, bands)
    above = lax.rem(m + members - 1, members)
    below = lax.rem(m + 1, members)

    barrier = pltpu.get_barrier_semaphore()
    for side in (left, right):
        for who in (above, m, below):
            pl.semaphore_signal(barrier, inc=1, device_id=(who, side), device_id_type=MESH)

    @pl.loop(1, members)
    def _(k):
        pl.semaphore_signal(
            barrier, inc=1, device_id=(lax.rem(m + k, members), b), device_id_type=MESH
        )

    thin = ((0, 40), (40, 40), (80, 16))

    def load(q):
        first, rows = thin[q]
        return pltpu.make_async_copy(
            x_hbm.at[0, pl.ds(first, rows)], xp.at[pl.ds(3 + first, rows)], in_sem.at[q]
        )

    for q in range(3):
        load(q).start()
    oc_copy = pltpu.make_async_copy(ocean_hbm.at[pl.ds(6 * m, 6)], oc, oc_sem)
    oc_copy.start()

    for ref in (xp, xe, yp, ye):
        ref[0:3] = jnp.zeros((3, C, W), BF16)
        ref[99:ROWS_IN] = jnp.zeros((ROWS_IN - 99, C, W), BF16)

    def thin_sends(q):
        return (
            pltpu.make_async_remote_copy(
                pack_r.at[q], fl1.at[q], s1.at[0, q], r1.at[0, q],
                device_id=(m, right), device_id_type=MESH,
            ),
            pltpu.make_async_remote_copy(
                pack_l.at[q], fr1.at[q], s1.at[1, q], r1.at[1, q],
                device_id=(m, left), device_id_type=MESH,
            ),
        )

    for q in range(3):
        load(q).wait()
        first, rows = thin[q]
        pack_r[q] = pack_thin(lambda k: xp[3 + first + k], rows, 3)
        pack_l[q] = pack_thin(lambda k: xp[3 + first + k], rows, 0)
        if q == 0:
            pl.semaphore_wait(barrier, members - 1 + 6)
        for copy in thin_sends(q):
            copy.start()

    band_matrix(lambda i: ak[i, :, 0], taps, bands1, OUT)
    for layer in range(2):
        up_t[layer] = (jnp.transpose(au[layer].astype(F32)) * 0.5).astype(BF16)
        down_t[layer] = ad[layer]
        gains[layer] = columns(ag[layer : layer + 1])
        scales[layer] = columns(asc[layer : layer + 1])
    up_t[2] = (jnp.transpose(ou[...].astype(F32)) * 0.5).astype(BF16)
    down_t[2] = od[...]
    gains[2] = columns(og[...])
    scales[2] = columns(osc[...])
    fw_t[...] = fw[...] * BF16(0.5)
    for s in range(2):
        fl_t[s] = jnp.transpose(fl[s].astype(F32)).astype(BF16)
    sw_t[...] = sw[...]
    bw_t[...] = jnp.transpose(bw[...].astype(F32)).astype(BF16)
    band_matrix(lambda i: ak[i, :, 1], taps, bands2, OUT)
    band_matrix(lambda i: okn[i], taps, bands3, 6)

    def thin_arrive(q):
        for copy in thin_sends(q):
            copy.wait()

    def thin_spread(p, q, odd):
        lane = lanes((C, W))
        for k in range(PAIR):
            at = 3 * (PAIR * odd + k)
            xe[3 + p * PAIR + k] = jnp.where(
                lane < W // 2, turn(fr1[q], -at), turn(fl1[q], -at - 3)
            )

    def sends(p):
        return (
            pltpu.make_async_remote_copy(
                pack2.at[p], fl2.at[p], s2.at[0, p], r2.at[0, p],
                device_id=(m, right), device_id_type=MESH,
            ),
            pltpu.make_async_remote_copy(
                pack2.at[p], fr2.at[p], s2.at[1, p], r2.at[1, p],
                device_id=(m, left), device_id_type=MESH,
            ),
        )

    def arrive(p):
        for copy in sends(p):
            copy.wait()
        both = joined_edges(fl2[p], fr2[p])
        for k in range(PAIR):
            ye[3 + p * PAIR + k] = turn(both, -SLOT * k)

    half = PAIR // 2

    def mlp_one(acc, p, c):
        add = branch(acc, c * half, half, up_t[0], down_t[0], gains[0])
        for k in range(half):
            row = 3 + p * PAIR + c * half + k
            yp[row] = (xp[row].astype(F32) + scales[0] * add[:, k * W : k * W + W]).astype(BF16)

    def mlp_two(acc, p, c):
        add = branch(acc, c * half, half, up_t[1], down_t[1], gains[1])
        rows = []
        for k in range(half):
            row = p * PAIR + c * half + k
            rows.append(
                (yp[3 + row].astype(F32) + scales[1] * add[:, k * W : k * W + W]).astype(BF16)
            )
            y2[row] = rows[k]
        out = half_gelu(
            jnp.dot(fw_t[...], jnp.concatenate(rows, 1), preferred_element_type=F32)
        ).astype(BF16)
        for k in range(half):
            flux[p * PAIR + c * half + k] = out[:, k * W : k * W + W]

    def finish_one(p):
        pack2[p] = pack_edges(lambda k: yp[3 + p * PAIR + k], PAIR)
        for copy in sends(p):
            copy.start()

    def flux_copy(piece):
        d = piece // 3
        return pltpu.make_async_remote_copy(
            flux.at[pl.ds(2 * piece, 2)], fluxes.at[m, pl.ds(2 * lax.rem(piece, 3), 2)],
            fs.at[d], fr.at[m], device_id=(d, b), device_id_type=MESH,
        )

    def flux_whole(k):
        return pltpu.make_async_remote_copy(
            flux.at[pl.ds(6 * k, 6)], fluxes.at[k], fs.at[k], fr.at[k],
            device_id=(k, b), device_id_type=MESH,
        )

    def finish_two(p):
        @pl.loop(half * p, jnp.minimum(half * p + half, 3 * members))
        def _(piece):
            @pl.when(piece // 3 != m)
            def _():
                flux_copy(piece).start()

    def step(mlp, acc, p, conv, next_acc, next_p):
        cells, edges, bands = conv
        for g in range(GROUPS):
            conv_group(cells, edges, bands, next_acc, next_p * PAIR, g)
            if g == 0:
                mlp(acc, p, 0)
            if g == 3:
                mlp(acc, p, 1)

    one = (xp, xe, bands1)
    two = (yp, ye, bands2)
    thin_arrive(0)
    thin_spread(0, 0, 0)
    thin_spread(1, 0, 1)
    for g in range(GROUPS):
        conv_group(*one, acc0, 0, g)

    @pl.loop(0, 2)
    def _(t):
        thin_arrive(t + 1)
        thin_spread(2 * t + 2, t + 1, 0)

        @pl.when(t == 1)
        def _():
            xe[99:ROWS_IN] = jnp.zeros((ROWS_IN - 99, C, W), BF16)

        step(mlp_one, acc0, 2 * t, one, acc1, 2 * t + 1)
        finish_one(2 * t)

        @pl.when(t == 0)
        def _():
            thin_spread(3, 1, 1)

        step(mlp_one, acc1, 2 * t + 1, one, acc0, 2 * t + 2)
        finish_one(2 * t + 1)

    kind = lax.rem(m, 3)
    start = (kind + 1) // 2
    stride = 1 - 2 * (kind // 2)

    def order(s):
        return lax.rem(start + stride * s + TILES, TILES)

    for p in range(3):
        arrive(p)
    step(mlp_one, acc0, TILES - 1, two, acc1, start)
    finish_one(TILES - 1)
    yp[99:ROWS_IN] = jnp.zeros((ROWS_IN - 99, C, W), BF16)

    @pl.loop(0, 2)
    def _(t):
        @pl.when(t == 0)
        def _():
            arrive(3)

        step(mlp_two, acc1, order(2 * t), two, acc0, order(2 * t + 1))
        finish_two(order(2 * t))

        @pl.when(t == 0)
        def _():
            arrive(4)
            ye[99:ROWS_IN] = jnp.zeros((ROWS_IN - 99, C, W), BF16)

        step(mlp_two, acc0, order(2 * t + 1), two, acc1, order(2 * t + 2))
        finish_two(order(2 * t + 1))

    for c in range(2):
        mlp_two(acc1, order(4), c)
    finish_two(order(4))

    fluxes[m] = flux[pl.ds(6 * m, 6)]

    @pl.loop(0, members)
    def _(k):
        @pl.when(k != m)
        def _():
            flux_whole(k).wait_recv()

    total = fluxes[0].astype(F32)
    for k in range(1, members):
        total = total + fluxes[k].astype(F32)
    low = (total * (1.0 / members)).astype(BF16)
    low = jnp.concatenate([low[k] for k in range(6)], 1)
    open_term = jnp.dot(fl_t[0], low, preferred_element_type=F32)
    ice_term = jnp.dot(fl_t[1], low, preferred_element_type=F32)
    oc_copy.wait()
    mid[...] = jnp.zeros(mid.shape, BF16)
    mide[...] = jnp.zeros(mide.shape, BF16)
    for k in range(6):
        sea = (1 - land[pl.ds(6 * m + k, 1), :]).astype(F32)
        ice = icem[pl.ds(6 * m + k, 1), :].astype(F32)
        at = slice(k * W, k * W + W)
        forcing = sea * ((1.0 - ice) * open_term[:, at] + ice * ice_term[:, at])
        mid[3 + k] = (oc[k].astype(F32) + forcing).astype(BF16)
    opack[...] = pack_edges(lambda k: mid[3 + k], 6)

    def ocean_rows_up():
        return pltpu.make_async_remote_copy(
            mid.at[pl.ds(3, 3)], orow_hi, os_.at[0], or_.at[0],
            device_id=(above, b), device_id_type=MESH,
        )

    def ocean_rows_down():
        return pltpu.make_async_remote_copy(
            mid.at[pl.ds(6, 3)], orow_lo, os_.at[1], or_.at[1],
            device_id=(below, b), device_id_type=MESH,
        )

    def edge_copy(step, side):
        who = (above, m, below)[step + 1]
        return pltpu.make_async_remote_copy(
            opack, oedge.at[1 - step, side], os_.at[2 + 2 * (step + 1) + side],
            or_.at[2 + 2 * (1 - step) + side],
            device_id=(who, (right, left)[side]), device_id_type=MESH,
        )

    has_above = m > 0
    has_below = m < members - 1

    def guarded(flag, act):
        if flag is None:
            act()
        else:
            pl.when(flag)(act)

    guards = {-1: has_above, 0: None, 1: has_below}
    pl.when(has_above)(lambda: ocean_rows_up().start())
    pl.when(has_below)(lambda: ocean_rows_down().start())
    for step in (0, -1, 1):
        for side in range(2):
            guarded(guards[step], lambda: edge_copy(step, side).start())

    pl.when(has_below)(lambda: ocean_rows_up().wait_recv())
    pl.when(has_above)(lambda: ocean_rows_down().wait_recv())
    for step in (0, 1, -1):
        for side in range(2):
            guarded(guards[-step], lambda: edge_copy(step, side).wait_recv())

    for step, first, count, at in ((-1, 3, 3, 0), (0, 0, 6, 3), (1, 0, 3, 9)):
        def fill(step=step, first=first, count=count, at=at):
            both = joined_edges(oedge[step + 1, 0], oedge[step + 1, 1])
            for k in range(count):
                mide[at + k] = turn(both, -SLOT * (first + k))

        guarded(guards[step], fill)

    pl.when(has_above)(lambda: ocean_rows_up().wait_send())
    pl.when(has_below)(lambda: ocean_rows_down().wait_send())
    for step in (0, -1, 1):
        for side in range(2):
            guarded(guards[step], lambda: edge_copy(step, side).wait_send())

    @pl.when(has_above)
    def _():
        mid[0:3] = orow_lo[...]

    @pl.when(has_below)
    def _():
        mid[9:12] = orow_hi[...]

    for g in range(GROUPS):
        out = jnp.dot(bands3[g], conv_part(mid, mide, g, 0), preferred_element_type=F32)
        acc0[0:6, GROUP * g : GROUP * g + GROUP, :] = out.reshape(6, GROUP, W)
    add = branch(acc0, 0, 6, up_t[2], down_t[2], gains[2])
    rows = []
    for k in range(6):
        sea = (1 - land[pl.ds(6 * m + k, 1), :]).astype(F32)
        new = ((mid[3 + k].astype(F32) + scales[2] * add[:, k * W : k * W + W]) * sea).astype(BF16)
        ocean_out[k] = new
        rows.append(new)
    top = jnp.dot(sw_t[...], jnp.concatenate(rows, 1), preferred_element_type=F32).astype(BF16)
    for k in range(6):
        surf[k] = top[:, k * W : k * W + W]

    mine = pl.ds(6 * m, 6)

    def surf_copy(d):
        return pltpu.make_async_remote_copy(
            surf, surfs.at[mine], ss.at[d], sr.at[m], device_id=(d, b), device_id_type=MESH
        )

    def surf_arrival(k):
        return pltpu.make_async_remote_copy(
            surf, surfs.at[pl.ds(6 * k, 6)], ss.at[k], sr.at[k],
            device_id=(k, b), device_id_type=MESH,
        )

    @pl.loop(1, members)
    def _(k):
        surf_copy(lax.rem(m + k, members)).start()

    surfs[mine] = surf[...]

    @pl.loop(1, members)
    def _(k):
        surf_arrival(lax.rem(m + k, members)).wait_recv()

    def store(t):
        return pltpu.make_async_copy(
            y2.at[pl.ds(16 * t, 16)], out_hbm.at[0, pl.ds(16 * t, 16)], out_sem.at[t]
        )

    @pl.loop(0, LAT // 16)
    def _(t):
        top = jnp.concatenate([surfs[16 * t + k] for k in range(16)], 1)
        add = jnp.dot(bw_t[...], top, preferred_element_type=F32)
        for k in range(16):
            row = 16 * t + k
            sea = (1 - land[pl.ds(row, 1), :]).astype(F32)
            y2[row] = (y2[row].astype(F32) + sea * add[:, k * W : k * W + W]).astype(BF16)
        store(t).start()

    @pl.loop(1, members)
    def _(k):
        surf_copy(lax.rem(m + k, members)).wait_send()
        flux_whole(lax.rem(m + k, members)).wait_send()

    @pl.loop(0, LAT // 16)
    def _(t):
        store(t).wait()


def local(
    atmos, ocean, land_mask, ice_mask, atm_kernel, atm_gain, atm_up, atm_down, atm_scale,
    flux_weight, flux_lift, ocn_kernel, ocn_gain, ocn_up, ocn_down, ocn_scale,
    surf_weight, back_weight,
):
    vmem = pl.BlockSpec(memory_space=pltpu.VMEM)
    hbm = pl.BlockSpec(memory_space=pl.ANY)
    dma = pltpu.SemaphoreType.DMA
    V = pltpu.VMEM
    field = V((ROWS_IN, C, W), BF16)
    packed = V((TILES, C, W), BF16)
    thin = V((3, C, W), BF16)
    return pl.pallas_call(
        coupled_kernel,
        out_shape=(
            jax.ShapeDtypeStruct((1, LAT, C, W), BF16),
            jax.ShapeDtypeStruct((6, C, W), BF16),
        ),
        in_specs=[hbm, hbm] + [vmem] * 16,
        out_specs=(hbm, vmem),
        scratch_shapes=[
            field, field, field, field, V((TILES * PAIR, C, W), BF16),
            V((GROUPS, GROUP * OUT, DEPTH), BF16), V((GROUPS, GROUP * OUT, DEPTH), BF16),
            V((GROUPS, GROUP * 6, DEPTH), BF16),
            V((PAIR, C, W), F32), V((PAIR, C, W), F32), V((W, W), F32),
            V((3, 384, C), BF16), V((3, C, 384), BF16), V((3, C, W), F32), V((3, C, W), F32),
            V((32, C), BF16), V((2, C, 32), BF16), V((8, C), BF16), V((C, 8), BF16),
            thin, thin, thin, thin, packed, packed, packed,
            V((TILES * PAIR, 32, W), BF16), V((16, 6, 32, W), BF16),
            V((6, C, W), BF16), V((WIN, C, W), BF16), V((WIN, C, W), BF16), V((C, W), BF16),
            V((3, C, W), BF16), V((3, C, W), BF16), V((3, 2, C, W), BF16),
            V((6, 8, W), BF16), V((LAT, 8, W), BF16),
            dma((3,)), dma, dma((LAT // 16,)),
            dma((2, 3)), dma((2, 3)), dma((2, TILES)), dma((2, TILES)),
            dma((16,)), dma((16,)), dma((8,)), dma((8,)), dma((16,)), dma((16,)),
        ],
        compiler_params=pltpu.CompilerParams(
            collective_id=0, has_side_effects=True, vmem_limit_bytes=60 * 2**20
        ),
        name="coupled",
    )(
        atmos, ocean, land_mask, ice_mask, jnp.transpose(atm_kernel, (1, 2, 0, 3)), atm_gain,
        atm_up, jnp.swapaxes(atm_down, 1, 2), atm_scale, flux_weight.T, flux_lift, ocn_kernel,
        ocn_gain.reshape(1, C), ocn_up, ocn_down.T, ocn_scale.reshape(1, C), surf_weight.T,
        back_weight,
    )


def solution(mesh):
    in_specs = (
        P("member", None, None, "lon"),
        P(None, None, "lon"),
        P(None, "lon"),
        P(None, "lon"),
    ) + (P(),) * 14
    out_specs = (P("member", None, None, "lon"), P("member", None, "lon"))
    return jax.shard_map(local, mesh=mesh, in_specs=in_specs, out_specs=out_specs, check_vma=False)
```

```python
import jax
import jax.numpy as jnp
from jax import lax
from jax.experimental import pallas as pl
from jax.experimental.pallas import tpu as pltpu
from jax.sharding import PartitionSpec as P

BF16 = jnp.bfloat16
F32 = jnp.float32
MESH = pl.DeviceIdType.MESH

C = 96
W = 128
LAT = 96
GROUP = 16
GROUPS = C // GROUP
OUT = 10
WIN = 16
PAIR = 2 * OUT
TILES = 5
SLOT = 6
FOLD = 32
TAPS = 7
DEPTH = TAPS * WIN * GROUP
ROWS_IN = 106
TANH_A = 2.0 * 0.7978845608028654
TANH_B = 8.0 * 0.7978845608028654 * 0.044715


def half_gelu(half):
    return half + half * jnp.tanh(half * (TANH_A + TANH_B * (half * half)))


def half_gelu_low(half):
    half = half.astype(BF16)
    return half + half * jnp.tanh(half * (BF16(TANH_A) + BF16(TANH_B) * (half * half)))


def lanes(shape):
    return lax.broadcasted_iota(jnp.int32, shape, len(shape) - 1)


def turn(v, shift):
    shift = shift % W
    return v if shift == 0 else pltpu.roll(v, shift, 1)


def band_matrix(kernel_of, taps, bands, outs):
    taps[...] = jnp.zeros(taps.shape, F32)
    for i in range(TAPS):
        taps[8 * i : 8 * i + TAPS, 0:C] = kernel_of(i)
    by_channel = jnp.transpose(taps[...])[0:C].astype(BF16)
    row = lax.broadcasted_iota(jnp.int32, (W, DEPTH), 0)
    lane = lanes((W, DEPTH))
    spread = (row % 8 == lane // (WIN * GROUP)) & (row // 8 == (lane % (WIN * GROUP)) // GROUP)
    wide = jnp.dot(by_channel, spread.astype(F32).astype(BF16), preferred_element_type=F32)
    crow = lax.broadcasted_iota(jnp.int32, (C, DEPTH), 0)
    wide = jnp.where(crow % GROUP == lanes((C, DEPTH)) % GROUP, wide, 0.0).astype(BF16)
    for g in range(GROUPS):
        base = wide[GROUP * g : GROUP * g + GROUP]
        for l in range(outs):
            bands[g, GROUP * l : GROUP * l + GROUP, :] = (
                base if l == 0 else pltpu.roll(base, GROUP * l, 1)
            )


def columns(vector_row):
    return jnp.transpose(jnp.broadcast_to(vector_row, (W, C)))


def shifted(cells, edge, d):
    if d == 0:
        return cells
    lane = lanes(cells.shape)
    if d > 0:
        return pltpu.roll(jnp.where(lane < d, edge, cells), W - d, 1)
    return pltpu.roll(jnp.where(lane >= W + d, edge, cells), -d, 1)


def conv_part(cells, edges, g, row):
    part = cells[pl.ds(row, WIN), GROUP * g : GROUP * g + GROUP, :].reshape(WIN * GROUP, W)
    edge = edges[pl.ds(row, WIN), GROUP * g : GROUP * g + GROUP, :].reshape(WIN * GROUP, W)
    return jnp.concatenate([shifted(part, edge, j - 3) for j in range(TAPS)], 0)


def conv_group(cells, edges, bands, acc, row, g):
    right = jnp.concatenate(
        [conv_part(cells, edges, g, row), conv_part(cells, edges, g, row + OUT)], 1
    )
    out = jnp.dot(bands[g], right, preferred_element_type=F32)
    for half in range(2):
        acc[OUT * half : OUT * half + OUT, GROUP * g : GROUP * g + GROUP, :] = out[
            :, half * W : half * W + W
        ].reshape(OUT, GROUP, W)


def normed(a, gain):
    center = a - jnp.mean(a, axis=0, keepdims=True)
    spread = jnp.mean(center * center, axis=0, keepdims=True)
    return (center * lax.rsqrt(spread + 1e-6) * gain).astype(BF16)


def branch(acc, first, count, up, down, gain):
    n = jnp.concatenate([normed(acc[first + k], gain) for k in range(count)], 1)
    hidden = half_gelu_low(jnp.dot(up, n, preferred_element_type=F32))
    return jnp.dot(down, hidden, preferred_element_type=F32)


def pack_edges(row_of, count):
    lane = lanes((C, W))
    slot = jnp.where(lane >= W - 3, 0, (lane + 3) // SLOT)
    packed = row_of(0)
    for k in range(1, count):
        packed = jnp.where(slot == k, turn(row_of(k), SLOT * k), packed)
    return packed


def pack_thin(row_of, count, shift):
    slot = lanes((C, W)) // 3
    packed = turn(row_of(0), shift)
    for k in range(1, count):
        packed = jnp.where(slot == k, turn(row_of(k), 3 * k + shift), packed)
    return packed


def joined_edges(from_left, from_right):
    lane = lanes((C, W))
    left_side = (lane >= W - 3) | ((lane < W - 5) & ((lane + 3) % SLOT < 3))
    return jnp.where(left_side, from_left, from_right)


def coupled_kernel(
    x_hbm, ocean_hbm, land_h, icem_h, ak_h, ag_h, au_h, ad_h, asc_h, fw_h, fl_h, okn_h, og_h,
    ou_h, od_h, osc_h, sw_h, bw_h,
    out_hbm, ocean_hbm_out,
    land, icem, ak, ag, au, ad, asc, fw, fl, okn, og, ou, od, osc, sw, bw, ocean_out,
    xp, xe, yp, ye, y2, bands1, bands2, bands3, acc0, acc1, taps, up_t, down_t, gains, scales,
    fw_t, fl_t, sw_t, bw_t,
    pack_r, pack_l, fl1, fr1, pack2, fl2, fr2, flux, fluxes, oc, mid, mide, opack,
    oedge, lowrows, low_lo, low_hi, surf, surfs,
    in_sem, oc_sem, out_sem, w_sem, oo_sem, s1, r1, s2, r2, fs, fr, os_, or_, ss, sr,
):
    m = lax.axis_index("member")
    b = lax.axis_index("lon")
    members = 16
    bands = 8
    right = lax.rem(b + 1, bands)
    left = lax.rem(b + bands - 1, bands)
    above = lax.rem(m + members - 1, members)
    below = lax.rem(m + 1, members)

    barrier = pltpu.get_barrier_semaphore()
    for side in (left, right):
        for who in (above, m, below):
            pl.semaphore_signal(barrier, inc=1, device_id=(who, side), device_id_type=MESH)

    @pl.loop(1, members)
    def _(k):
        pl.semaphore_signal(
            barrier, inc=1, device_id=(lax.rem(m + k, members), b), device_id_type=MESH
        )

    thin = ((0, 40), (40, 40), (80, 16))

    def load(q):
        first, rows = thin[q]
        return pltpu.make_async_copy(
            x_hbm.at[0, pl.ds(first, rows)], xp.at[pl.ds(3 + first, rows)], in_sem.at[q]
        )

    for q in range(3):
        load(q).start()
    pairs = (
        (ak_h, ak), (au_h, au), (ad_h, ad), (ag_h, ag), (asc_h, asc), (fw_h, fw), (fl_h, fl),
        (okn_h, okn), (og_h, og), (ou_h, ou), (od_h, od), (osc_h, osc), (sw_h, sw), (bw_h, bw),
        (land_h, land), (icem_h, icem),
    )
    small = [pltpu.make_async_copy(a, c, w_sem.at[i]) for i, (a, c) in enumerate(pairs)]
    for copy in small:
        copy.start()
    base = jnp.minimum(jnp.maximum(6 * m - 3, 0), LAT - 12)
    oc_copy = pltpu.make_async_copy(ocean_hbm.at[pl.ds(base, 12)], oc, oc_sem)
    oc_copy.start()

    for ref in (xp, xe, yp, ye):
        ref[0:3] = jnp.zeros((3, C, W), BF16)
        ref[99:ROWS_IN] = jnp.zeros((ROWS_IN - 99, C, W), BF16)

    def thin_sends(q):
        return (
            pltpu.make_async_remote_copy(
                pack_r.at[q], fl1.at[q], s1.at[0, q], r1.at[0, q],
                device_id=(m, right), device_id_type=MESH,
            ),
            pltpu.make_async_remote_copy(
                pack_l.at[q], fr1.at[q], s1.at[1, q], r1.at[1, q],
                device_id=(m, left), device_id_type=MESH,
            ),
        )

    for q in range(3):
        load(q).wait()
        first, rows = thin[q]
        pack_r[q] = pack_thin(lambda k: xp[3 + first + k], rows, 3)
        pack_l[q] = pack_thin(lambda k: xp[3 + first + k], rows, 0)
        if q == 0:
            pl.semaphore_wait(barrier, members - 1 + 6)
        for copy in thin_sends(q):
            copy.start()

    for copy in small:
        copy.wait()
    band_matrix(lambda i: ak[i, :, 0], taps, bands1, OUT)
    for layer in range(2):
        up_t[layer] = (jnp.transpose(au[layer].astype(F32)) * 0.5).astype(BF16)
        down_t[layer] = ad[layer]
        gains[layer] = columns(ag[layer : layer + 1])
        scales[layer] = columns(asc[layer : layer + 1])
    up_t[2] = (jnp.transpose(ou[...].astype(F32)) * 0.5).astype(BF16)
    down_t[2] = od[...]
    gains[2] = columns(og[...])
    scales[2] = columns(osc[...])
    fw_t[...] = fw[...] * BF16(0.5)
    for s in range(2):
        fl_t[s] = jnp.transpose(fl[s].astype(F32)).astype(BF16)
    sw_t[...] = sw[...]
    bw_t[...] = jnp.transpose(bw[...].astype(F32)).astype(BF16)
    band_matrix(lambda i: ak[i, :, 1], taps, bands2, OUT)
    band_matrix(lambda i: okn[i], taps, bands3, 6)

    def thin_arrive(q):
        for copy in thin_sends(q):
            copy.wait()

    def thin_spread(p, q, odd):
        lane = lanes((C, W))
        for k in range(min(PAIR, LAT - p * PAIR)):
            at = 3 * (PAIR * odd + k)
            xe[3 + p * PAIR + k] = jnp.where(
                lane < W // 2, turn(fr1[q], -at), turn(fl1[q], -at - 3)
            )

    def sends(p):
        return (
            pltpu.make_async_remote_copy(
                pack2.at[p], fl2.at[p], s2.at[0, p], r2.at[0, p],
                device_id=(m, right), device_id_type=MESH,
            ),
            pltpu.make_async_remote_copy(
                pack2.at[p], fr2.at[p], s2.at[1, p], r2.at[1, p],
                device_id=(m, left), device_id_type=MESH,
            ),
        )

    def arrive(p):
        for copy in sends(p):
            copy.wait()
        both = joined_edges(fl2[p], fr2[p])
        for k in range(PAIR):
            ye[3 + p * PAIR + k] = turn(both, -SLOT * k)

    half = PAIR // 2

    def mlp_one(acc, p, c):
        add = branch(acc, c * half, half, up_t[0], down_t[0], gains[0])
        for k in range(half):
            row = 3 + p * PAIR + c * half + k
            yp[row] = (xp[row].astype(F32) + scales[0] * add[:, k * W : k * W + W]).astype(BF16)

    def mlp_two(acc, p, c):
        add = branch(acc, c * half, half, up_t[1], down_t[1], gains[1])
        rows = []
        for k in range(half):
            row = p * PAIR + c * half + k
            rows.append(
                (yp[3 + row].astype(F32) + scales[1] * add[:, k * W : k * W + W]).astype(BF16)
            )
            y2[row] = rows[k]
        out = half_gelu(
            jnp.dot(fw_t[...], jnp.concatenate(rows, 1), preferred_element_type=F32)
        ).astype(BF16)
        for k in range(half):
            flux[p * PAIR + c * half + k] = out[:, k * W : k * W + W]

    def finish_one(p):
        pack2[p] = pack_edges(lambda k: yp[3 + p * PAIR + k], PAIR)
        for copy in sends(p):
            copy.start()

    def flux_copy(piece):
        d = piece // 3
        return pltpu.make_async_remote_copy(
            flux.at[pl.ds(2 * piece, 2)], fluxes.at[m, pl.ds(2 * lax.rem(piece, 3), 2)],
            fs.at[d], fr.at[m], device_id=(d, b), device_id_type=MESH,
        )

    def flux_whole(k):
        return pltpu.make_async_remote_copy(
            flux.at[pl.ds(6 * k, 6)], fluxes.at[k], fs.at[k], fr.at[k],
            device_id=(k, b), device_id_type=MESH,
        )

    def finish_two(p, first=0, count=half):
        @pl.loop(half * p + first, jnp.minimum(half * p + first + count, 3 * members))
        def _(piece):
            @pl.when(piece // 3 != m)
            def _():
                flux_copy(piece).start()

    def step(mlp, acc, p, conv, next_acc, next_p):
        cells, edges, bands = conv
        for g in range(GROUPS):
            conv_group(cells, edges, bands, next_acc, next_p * PAIR, g)
            if g == 0:
                mlp(acc, p, 0)
            if g == 3:
                mlp(acc, p, 1)

    one = (xp, xe, bands1)
    two = (yp, ye, bands2)
    thin_arrive(0)
    thin_spread(0, 0, 0)
    thin_spread(1, 0, 1)
    for g in range(GROUPS):
        conv_group(*one, acc0, 0, g)

    for p in range(TILES - 1):
        if p % 2 == 0:
            thin_arrive(p // 2 + 1)
        if p + 2 < TILES:
            thin_spread(p + 2, (p + 2) // 2, p % 2)
        acc, next_acc = (acc0, acc1) if p % 2 == 0 else (acc1, acc0)
        step(mlp_one, acc, p, one, next_acc, p + 1)
        finish_one(p)

    kind = lax.rem(m, 3)
    start = (kind + 1) // 2
    stride = 1 - 2 * (kind // 2)

    def order(s):
        return lax.rem(start + stride * s + TILES, TILES)

    for p in range(3):
        arrive(p)
    step(mlp_one, acc0, TILES - 1, two, acc1, start)
    finish_one(TILES - 1)
    yp[99:ROWS_IN] = jnp.zeros((ROWS_IN - 99, C, W), BF16)

    @pl.loop(0, 2)
    def _(t):
        @pl.when(t == 0)
        def _():
            arrive(3)

        step(mlp_two, acc1, order(2 * t), two, acc0, order(2 * t + 1))
        finish_two(order(2 * t))

        @pl.when(t == 0)
        def _():
            arrive(4)
            ye[99:ROWS_IN] = jnp.zeros((ROWS_IN - 99, C, W), BF16)

        step(mlp_two, acc0, order(2 * t + 1), two, acc1, order(2 * t + 2))
        finish_two(order(2 * t + 1))

    for c in range(2):
        mlp_two(acc1, order(4), c)
        finish_two(order(4), c * (half // 2), half // 2)

    fluxes[m] = flux[pl.ds(6 * m, 6)]

    @pl.loop(0, members)
    def _(k):
        @pl.when(k != m)
        def _():
            flux_whole(k).wait_recv()

    total = fluxes[0].astype(F32)
    for k in range(1, members):
        total = total + fluxes[k].astype(F32)
    lowrows[...] = (total * (1.0 / members)).astype(BF16)

    def rows_up():
        return pltpu.make_async_remote_copy(
            lowrows.at[pl.ds(0, 3)], low_hi, os_.at[0], or_.at[0],
            device_id=(above, b), device_id_type=MESH,
        )

    def rows_down():
        return pltpu.make_async_remote_copy(
            lowrows.at[pl.ds(3, 3)], low_lo, os_.at[1], or_.at[1],
            device_id=(below, b), device_id_type=MESH,
        )

    def edge_copy(step, side):
        who = (above, m, below)[step + 1]
        return pltpu.make_async_remote_copy(
            opack, oedge.at[1 - step, side], os_.at[2 + 2 * (step + 1) + side],
            or_.at[2 + 2 * (1 - step) + side],
            device_id=(who, (right, left)[side]), device_id_type=MESH,
        )

    def force(low, first):
        rows = len(low)
        low = jnp.concatenate(low, 1)
        open_term = jnp.dot(fl_t[0], low, preferred_element_type=F32)
        ice_term = jnp.dot(fl_t[1], low, preferred_element_type=F32)
        for k in range(rows):
            row = 6 * m - 3 + first + k
            sea = (1 - land[pl.ds(row, 1), :]).astype(F32)
            ice = icem[pl.ds(row, 1), :].astype(F32)
            at = slice(k * W, k * W + W)
            forcing = sea * ((1.0 - ice) * open_term[:, at] + ice * ice_term[:, at])
            mid[first + k] = (oc[row - base].astype(F32) + forcing).astype(BF16)

    has_above = m > 0
    has_below = m < members - 1

    def guarded(flag, act):
        if flag is None:
            act()
        else:
            pl.when(flag)(act)

    guards = {-1: has_above, 0: None, 1: has_below}
    pl.when(has_above)(lambda: rows_up().start())
    pl.when(has_below)(lambda: rows_down().start())
    oc_copy.wait()
    mid[...] = jnp.zeros(mid.shape, BF16)
    mide[...] = jnp.zeros(mide.shape, BF16)
    force([lowrows[k] for k in range(6)], 3)
    edge = pack_edges(lambda k: mid[3 + k], 6)
    fold = turn(edge[0:FOLD], 3)
    for third in range(1, 3):
        fold = jnp.where(
            lanes((FOLD, W)) < 36 * third, fold,
            turn(edge[FOLD * third : FOLD * third + FOLD], 3 + 36 * third),
        )
    opack[...] = fold
    for step in (-1, 1, 0):
        for side in range(2):
            guarded(guards[step], lambda: edge_copy(step, side).start())

    @pl.when(has_below)
    def _():
        rows_up().wait_recv()
        force([low_hi[k] for k in range(3)], 9)

    @pl.when(has_above)
    def _():
        rows_down().wait_recv()
        force([low_lo[k] for k in range(3)], 0)

    def unfold(packed):
        return jnp.concatenate([turn(packed, -3 - 36 * third) for third in range(3)], 0)

    for view, first, count, at in ((0, 0, 6, 3), (-1, 3, 3, 0), (1, 0, 3, 9)):
        def fill(view=view, first=first, count=count, at=at):
            for side in range(2):
                edge_copy(-view, side).wait_recv()
            both = joined_edges(unfold(oedge[view + 1, 0]), unfold(oedge[view + 1, 1]))
            for k in range(count):
                mide[at + k] = turn(both, -SLOT * (first + k))

        guarded(guards[view], fill)

    for g in range(GROUPS):
        out = jnp.dot(bands3[g], conv_part(mid, mide, g, 0), preferred_element_type=F32)
        acc0[0:6, GROUP * g : GROUP * g + GROUP, :] = out.reshape(6, GROUP, W)
    add = branch(acc0, 0, 6, up_t[2], down_t[2], gains[2])
    rows = []
    for k in range(6):
        sea = (1 - land[pl.ds(6 * m + k, 1), :]).astype(F32)
        new = ((mid[3 + k].astype(F32) + scales[2] * add[:, k * W : k * W + W]) * sea).astype(BF16)
        ocean_out[k] = new
        rows.append(new)
    top = jnp.dot(sw_t[...], jnp.concatenate(rows, 1), preferred_element_type=F32).astype(BF16)
    for k in range(6):
        surf[k] = top[:, k * W : k * W + W]

    mine = pl.ds(6 * m, 6)

    def surf_copy(d):
        return pltpu.make_async_remote_copy(
            surf, surfs.at[mine], ss.at[d], sr.at[m], device_id=(d, b), device_id_type=MESH
        )

    def surf_arrival(k):
        return pltpu.make_async_remote_copy(
            surf, surfs.at[pl.ds(6 * k, 6)], ss.at[k], sr.at[k],
            device_id=(k, b), device_id_type=MESH,
        )

    @pl.loop(1, members)
    def _(k):
        surf_copy(lax.rem(m + k, members)).start()

    surfs[mine] = surf[...]

    @pl.loop(1, members)
    def _(k):
        surf_arrival(lax.rem(m + k, members)).wait_recv()

    ocean_store = pltpu.make_async_copy(ocean_out, ocean_hbm_out, oo_sem)
    ocean_store.start()

    def store(t):
        return pltpu.make_async_copy(
            y2.at[pl.ds(16 * t, 16)], out_hbm.at[0, pl.ds(16 * t, 16)], out_sem.at[t]
        )

    @pl.loop(0, LAT // 16)
    def _(t):
        top = jnp.concatenate([surfs[16 * t + k] for k in range(16)], 1)
        add = jnp.dot(bw_t[...], top, preferred_element_type=F32)
        for k in range(16):
            row = 16 * t + k
            sea = (1 - land[pl.ds(row, 1), :]).astype(F32)
            y2[row] = (y2[row].astype(F32) + sea * add[:, k * W : k * W + W]).astype(BF16)
        store(t).start()

    pl.when(has_above)(lambda: rows_up().wait_send())
    pl.when(has_below)(lambda: rows_down().wait_send())
    for step in (0, -1, 1):
        for side in range(2):
            guarded(guards[step], lambda: edge_copy(step, side).wait_send())

    @pl.loop(1, members)
    def _(k):
        surf_copy(lax.rem(m + k, members)).wait_send()
        flux_whole(lax.rem(m + k, members)).wait_send()

    @pl.loop(0, LAT // 16)
    def _(t):
        store(t).wait()

    ocean_store.wait()


def local(
    atmos, ocean, land_mask, ice_mask, atm_kernel, atm_gain, atm_up, atm_down, atm_scale,
    flux_weight, flux_lift, ocn_kernel, ocn_gain, ocn_up, ocn_down, ocn_scale,
    surf_weight, back_weight,
):
    hbm = pl.BlockSpec(memory_space=pl.ANY)
    dma = pltpu.SemaphoreType.DMA
    V = pltpu.VMEM
    field = V((ROWS_IN, C, W), BF16)
    packed = V((TILES, C, W), BF16)
    thin = V((3, C, W), BF16)
    small = (
        land_mask, ice_mask, jnp.transpose(atm_kernel, (1, 2, 0, 3)), atm_gain, atm_up,
        jnp.swapaxes(atm_down, 1, 2), atm_scale, flux_weight.T, flux_lift, ocn_kernel,
        ocn_gain.reshape(1, C), ocn_up, ocn_down.T, ocn_scale.reshape(1, C), surf_weight.T,
        back_weight,
    )
    return pl.pallas_call(
        coupled_kernel,
        out_shape=(
            jax.ShapeDtypeStruct((1, LAT, C, W), BF16),
            jax.ShapeDtypeStruct((6, C, W), BF16),
        ),
        in_specs=[hbm] * 18,
        out_specs=(hbm, hbm),
        scratch_shapes=[
            *[V(a.shape, a.dtype) for a in small], V((6, C, W), BF16),
            field, field, field, field, V((TILES * PAIR, C, W), BF16),
            V((GROUPS, GROUP * OUT, DEPTH), BF16), V((GROUPS, GROUP * OUT, DEPTH), BF16),
            V((GROUPS, GROUP * 6, DEPTH), BF16),
            V((PAIR, C, W), F32), V((PAIR, C, W), F32), V((W, W), F32),
            V((3, 384, C), BF16), V((3, C, 384), BF16), V((3, C, W), F32), V((3, C, W), F32),
            V((32, C), BF16), V((2, C, 32), BF16), V((8, C), BF16), V((C, 8), BF16),
            thin, thin, thin, thin, packed, packed, packed,
            V((TILES * PAIR, 32, W), BF16), V((16, 6, 32, W), BF16),
            V((12, C, W), BF16), V((WIN, C, W), BF16), V((WIN, C, W), BF16), V((FOLD, W), BF16),
            V((3, 2, FOLD, W), BF16),
            V((6, 32, W), BF16), V((3, 32, W), BF16), V((3, 32, W), BF16),
            V((6, 8, W), BF16), V((LAT, 8, W), BF16),
            dma((3,)), dma, dma((LAT // 16,)), dma((16,)), dma,
            dma((2, 3)), dma((2, 3)), dma((2, TILES)), dma((2, TILES)),
            dma((16,)), dma((16,)), dma((8,)), dma((8,)), dma((16,)), dma((16,)),
        ],
        compiler_params=pltpu.CompilerParams(
            collective_id=0, has_side_effects=True, vmem_limit_bytes=60 * 2**20
        ),
        name="coupled",
    )(atmos, ocean, *small)


def solution(mesh):
    in_specs = (
        P("member", None, None, "lon"),
        P(None, None, "lon"),
        P(None, "lon"),
        P(None, "lon"),
    ) + (P(),) * 14
    out_specs = (P("member", None, None, "lon"), P("member", None, "lon"))
    return jax.shard_map(local, mesh=mesh, in_specs=in_specs, out_specs=out_specs, check_vma=False)
```

```python
import jax
import jax.numpy as jnp
from jax import lax
from jax.experimental import pallas as pl
from jax.experimental.pallas import tpu as pltpu
from jax.sharding import PartitionSpec as P

BF16 = jnp.bfloat16
F32 = jnp.float32
MESH = pl.DeviceIdType.MESH

C = 96
W = 128
LAT = 96
GROUP = 16
GROUPS = C // GROUP
OUT = 10
WIN = 16
PAIR = 2 * OUT
TILES = 5
SLOT = 6
FOLD = 32
CHUNK = 32
TAPS = 7
DEPTH = TAPS * WIN * GROUP
ROWS_IN = 106
TANH_A = 2.0 * 0.7978845608028654
TANH_B = 8.0 * 0.7978845608028654 * 0.044715


def half_gelu(half):
    return half + half * jnp.tanh(half * (TANH_A + TANH_B * (half * half)))


def half_gelu_low(half):
    half = half.astype(BF16)
    return half + half * jnp.tanh(half * (BF16(TANH_A) + BF16(TANH_B) * (half * half)))


def lanes(shape):
    return lax.broadcasted_iota(jnp.int32, shape, len(shape) - 1)


def turn(v, shift):
    shift = shift % W
    return v if shift == 0 else pltpu.roll(v, shift, 1)


def band_matrix(kernel_of, taps, bands, outs):
    taps[...] = jnp.zeros(taps.shape, F32)
    for i in range(TAPS):
        taps[8 * i : 8 * i + TAPS, 0:C] = kernel_of(i)
    by_channel = jnp.transpose(taps[...])[0:C].astype(BF16)
    row = lax.broadcasted_iota(jnp.int32, (W, DEPTH), 0)
    lane = lanes((W, DEPTH))
    spread = (row % 8 == lane // (WIN * GROUP)) & (row // 8 == (lane % (WIN * GROUP)) // GROUP)
    wide = jnp.dot(by_channel, spread.astype(F32).astype(BF16), preferred_element_type=F32)
    crow = lax.broadcasted_iota(jnp.int32, (C, DEPTH), 0)
    wide = jnp.where(crow % GROUP == lanes((C, DEPTH)) % GROUP, wide, 0.0).astype(BF16)
    for g in range(GROUPS):
        base = wide[GROUP * g : GROUP * g + GROUP]
        for l in range(outs):
            bands[g, GROUP * l : GROUP * l + GROUP, :] = (
                base if l == 0 else pltpu.roll(base, GROUP * l, 1)
            )


def columns(vector_row):
    return jnp.transpose(jnp.broadcast_to(vector_row, (W, C)))


def shifted(cells, edge, d):
    if d == 0:
        return cells
    lane = lanes(cells.shape)
    if d > 0:
        return pltpu.roll(jnp.where(lane < d, edge, cells), W - d, 1)
    return pltpu.roll(jnp.where(lane >= W + d, edge, cells), -d, 1)


def conv_part(cells, edges, g, row):
    part = cells[pl.ds(row, WIN), GROUP * g : GROUP * g + GROUP, :].reshape(WIN * GROUP, W)
    edge = edges[pl.ds(row, WIN), GROUP * g : GROUP * g + GROUP, :].reshape(WIN * GROUP, W)
    return jnp.concatenate([shifted(part, edge, j - 3) for j in range(TAPS)], 0)


def conv_group(cells, edges, bands, acc, row, g):
    right = jnp.concatenate(
        [conv_part(cells, edges, g, row), conv_part(cells, edges, g, row + OUT)], 1
    )
    out = jnp.dot(bands[g], right, preferred_element_type=F32)
    for half in range(2):
        acc[OUT * half : OUT * half + OUT, GROUP * g : GROUP * g + GROUP, :] = out[
            :, half * W : half * W + W
        ].reshape(OUT, GROUP, W)


def normed(a, gain):
    center = a - jnp.mean(a, axis=0, keepdims=True)
    spread = jnp.mean(center * center, axis=0, keepdims=True)
    return (center * lax.rsqrt(spread + 1e-6) * gain).astype(BF16)


def branch(acc, first, count, up, down, gain):
    n = jnp.concatenate([normed(acc[first + k], gain) for k in range(count)], 1)
    hidden = half_gelu_low(jnp.dot(up, n, preferred_element_type=F32))
    return jnp.dot(down, hidden, preferred_element_type=F32)


def pack_edges(row_of, count):
    lane = lanes((C, W))
    slot = jnp.where(lane >= W - 3, 0, (lane + 3) // SLOT)
    packed = row_of(0)
    for k in range(1, count):
        packed = jnp.where(slot == k, turn(row_of(k), SLOT * k), packed)
    return packed


def pack_thin(row_of, count, shift):
    slot = lanes((C, W)) // 3
    packed = turn(row_of(0), shift)
    for k in range(1, count):
        packed = jnp.where(slot == k, turn(row_of(k), 3 * k + shift), packed)
    return packed


def joined_edges(from_left, from_right):
    lane = lanes((C, W))
    left_side = (lane >= W - 3) | ((lane < W - 5) & ((lane + 3) % SLOT < 3))
    return jnp.where(left_side, from_left, from_right)


def coupled_kernel(
    x_hbm, ocean_hbm, land_h, icem_h, ak_h, ag_h, au_h, ad_h, asc_h, fw_h, fl_h, okn_h, og_h,
    ou_h, od_h, osc_h, sw_h,
    y_hbm, ocean_hbm_out, surf_hbm,
    land, icem, ak, ag, au, ad, asc, fw, fl, okn, og, ou, od, osc, sw, ocean_out,
    xp, xe, yp, ye, y2, bands1, bands2, bands3, acc0, acc1, taps, up_t, down_t, gains, scales,
    fw_t, fl_t, sw_t,
    pack_r, pack_l, fl1, fr1, pack2, fl2, fr2, flux, fluxes, oc, mid, mide, opack,
    oedge, lowrows, low_lo, low_hi, surf, surfs,
    in_sem, oc_sem, out_sem, w_sem, s1, r1, s2, r2, fs, fr, os_, or_, ss, sr,
):
    m = lax.axis_index("member")
    b = lax.axis_index("lon")
    members = 16
    bands = 8
    right = lax.rem(b + 1, bands)
    left = lax.rem(b + bands - 1, bands)
    above = lax.rem(m + members - 1, members)
    below = lax.rem(m + 1, members)

    barrier = pltpu.get_barrier_semaphore()
    for side in (left, right):
        for who in (above, m, below):
            pl.semaphore_signal(barrier, inc=1, device_id=(who, side), device_id_type=MESH)

    @pl.loop(1, members)
    def _(k):
        pl.semaphore_signal(
            barrier, inc=1, device_id=(lax.rem(m + k, members), b), device_id_type=MESH
        )

    thin = ((0, 40), (40, 40), (80, 16))

    def load(q):
        first, rows = thin[q]
        return pltpu.make_async_copy(
            x_hbm.at[0, pl.ds(first, rows)], xp.at[pl.ds(3 + first, rows)], in_sem.at[q]
        )

    for q in range(3):
        load(q).start()
    pairs = (
        (ak_h, ak), (au_h, au), (ad_h, ad), (ag_h, ag), (asc_h, asc), (fw_h, fw), (fl_h, fl),
        (okn_h, okn), (og_h, og), (ou_h, ou), (od_h, od), (osc_h, osc), (sw_h, sw),
        (land_h, land), (icem_h, icem),
    )
    small = [pltpu.make_async_copy(a, c, w_sem.at[i]) for i, (a, c) in enumerate(pairs)]
    for copy in small:
        copy.start()
    base = jnp.minimum(jnp.maximum(6 * m - 3, 0), LAT - 12)
    oc_copy = pltpu.make_async_copy(ocean_hbm.at[pl.ds(base, 12)], oc, oc_sem)
    oc_copy.start()

    for ref in (xp, xe, yp, ye):
        ref[0:3] = jnp.zeros((3, C, W), BF16)
        ref[99:ROWS_IN] = jnp.zeros((ROWS_IN - 99, C, W), BF16)

    def thin_sends(q):
        return (
            pltpu.make_async_remote_copy(
                pack_r.at[q], fl1.at[q], s1.at[0, q], r1.at[0, q],
                device_id=(m, right), device_id_type=MESH,
            ),
            pltpu.make_async_remote_copy(
                pack_l.at[q], fr1.at[q], s1.at[1, q], r1.at[1, q],
                device_id=(m, left), device_id_type=MESH,
            ),
        )

    for q in range(3):
        load(q).wait()
        first, rows = thin[q]
        pack_r[q] = pack_thin(lambda k: xp[3 + first + k], rows, 3)
        pack_l[q] = pack_thin(lambda k: xp[3 + first + k], rows, 0)
        if q == 0:
            pl.semaphore_wait(barrier, members - 1 + 6)
        for copy in thin_sends(q):
            copy.start()

    for copy in small:
        copy.wait()
    band_matrix(lambda i: ak[i, :, 0], taps, bands1, OUT)
    for layer in range(2):
        up_t[layer] = (jnp.transpose(au[layer].astype(F32)) * 0.5).astype(BF16)
        down_t[layer] = ad[layer]
        gains[layer] = columns(ag[layer : layer + 1])
        scales[layer] = columns(asc[layer : layer + 1])
    up_t[2] = (jnp.transpose(ou[...].astype(F32)) * 0.5).astype(BF16)
    down_t[2] = od[...]
    gains[2] = columns(og[...])
    scales[2] = columns(osc[...])
    fw_t[...] = fw[...] * BF16(0.5)
    for s in range(2):
        fl_t[s] = jnp.transpose(fl[s].astype(F32)).astype(BF16)
    sw_t[...] = sw[...]
    band_matrix(lambda i: ak[i, :, 1], taps, bands2, OUT)
    band_matrix(lambda i: okn[i], taps, bands3, 6)

    def thin_arrive(q):
        for copy in thin_sends(q):
            copy.wait()

    def thin_spread(p, q, odd):
        lane = lanes((C, W))
        for k in range(min(PAIR, LAT - p * PAIR)):
            at = 3 * (PAIR * odd + k)
            xe[3 + p * PAIR + k] = jnp.where(
                lane < W // 2, turn(fr1[q], -at), turn(fl1[q], -at - 3)
            )

    def sends(p):
        return (
            pltpu.make_async_remote_copy(
                pack2.at[p], fl2.at[p], s2.at[0, p], r2.at[0, p],
                device_id=(m, right), device_id_type=MESH,
            ),
            pltpu.make_async_remote_copy(
                pack2.at[p], fr2.at[p], s2.at[1, p], r2.at[1, p],
                device_id=(m, left), device_id_type=MESH,
            ),
        )

    def arrive(p):
        for copy in sends(p):
            copy.wait()
        both = joined_edges(fl2[p], fr2[p])
        for k in range(PAIR):
            ye[3 + p * PAIR + k] = turn(both, -SLOT * k)

    half = PAIR // 2

    def mlp_one(acc, p, c):
        add = branch(acc, c * half, half, up_t[0], down_t[0], gains[0])
        for k in range(half):
            row = 3 + p * PAIR + c * half + k
            yp[row] = (xp[row].astype(F32) + scales[0] * add[:, k * W : k * W + W]).astype(BF16)

    def mlp_two(acc, p, c):
        add = branch(acc, c * half, half, up_t[1], down_t[1], gains[1])
        rows = []
        for k in range(half):
            row = p * PAIR + c * half + k
            rows.append(
                (yp[3 + row].astype(F32) + scales[1] * add[:, k * W : k * W + W]).astype(BF16)
            )
            y2[row] = rows[k]
        out = half_gelu(
            jnp.dot(fw_t[...], jnp.concatenate(rows, 1), preferred_element_type=F32)
        ).astype(BF16)
        for k in range(half):
            flux[p * PAIR + c * half + k] = out[:, k * W : k * W + W]

    def finish_one(p):
        pack2[p] = pack_edges(lambda k: yp[3 + p * PAIR + k], PAIR)
        for copy in sends(p):
            copy.start()

    def flux_copy(piece):
        d = piece // 3
        return pltpu.make_async_remote_copy(
            flux.at[pl.ds(2 * piece, 2)], fluxes.at[m, pl.ds(2 * lax.rem(piece, 3), 2)],
            fs.at[d], fr.at[m], device_id=(d, b), device_id_type=MESH,
        )

    def flux_whole(k):
        return pltpu.make_async_remote_copy(
            flux.at[pl.ds(6 * k, 6)], fluxes.at[k], fs.at[k], fr.at[k],
            device_id=(k, b), device_id_type=MESH,
        )

    def finish_two(p, first=0, count=half):
        @pl.loop(half * p + first, jnp.minimum(half * p + first + count, 3 * members))
        def _(piece):
            @pl.when(piece // 3 != m)
            def _():
                flux_copy(piece).start()

    def step(mlp, acc, p, conv, next_acc, next_p):
        cells, edges, bands = conv
        for g in range(GROUPS):
            conv_group(cells, edges, bands, next_acc, next_p * PAIR, g)
            if g == 0:
                mlp(acc, p, 0)
            if g == 3:
                mlp(acc, p, 1)

    one = (xp, xe, bands1)
    two = (yp, ye, bands2)
    thin_arrive(0)
    thin_spread(0, 0, 0)
    thin_spread(1, 0, 1)
    for g in range(GROUPS):
        conv_group(*one, acc0, 0, g)

    for p in range(TILES - 1):
        if p % 2 == 0:
            thin_arrive(p // 2 + 1)
        if p + 2 < TILES:
            thin_spread(p + 2, (p + 2) // 2, p % 2)
        acc, next_acc = (acc0, acc1) if p % 2 == 0 else (acc1, acc0)
        step(mlp_one, acc, p, one, next_acc, p + 1)
        finish_one(p)

    kind = lax.rem(m, 3)
    start = (kind + 1) // 2
    stride = 1 - 2 * (kind // 2)

    def order(s):
        return lax.rem(start + stride * s + TILES, TILES)

    for p in range(3):
        arrive(p)
    step(mlp_one, acc0, TILES - 1, two, acc1, start)
    finish_one(TILES - 1)
    yp[99:ROWS_IN] = jnp.zeros((ROWS_IN - 99, C, W), BF16)

    @pl.loop(0, 2)
    def _(t):
        @pl.when(t == 0)
        def _():
            arrive(3)

        step(mlp_two, acc1, order(2 * t), two, acc0, order(2 * t + 1))
        finish_two(order(2 * t))

        @pl.when(t == 0)
        def _():
            arrive(4)
            ye[99:ROWS_IN] = jnp.zeros((ROWS_IN - 99, C, W), BF16)

        step(mlp_two, acc0, order(2 * t + 1), two, acc1, order(2 * t + 2))
        finish_two(order(2 * t + 1))

    for c in range(2):
        mlp_two(acc1, order(4), c)
        finish_two(order(4), c * (half // 2), half // 2)

    y_store = pltpu.make_async_copy(y2.at[pl.ds(0, LAT)], y_hbm, out_sem.at[0])
    y_store.start()

    fluxes[m] = flux[pl.ds(6 * m, 6)]

    @pl.loop(0, members)
    def _(k):
        @pl.when(k != m)
        def _():
            flux_whole(k).wait_recv()

    total = fluxes[0].astype(F32)
    for k in range(1, members):
        total = total + fluxes[k].astype(F32)
    lowrows[...] = (total * (1.0 / members)).astype(BF16)

    def rows_up():
        return pltpu.make_async_remote_copy(
            lowrows.at[pl.ds(0, 3)], low_hi, os_.at[0], or_.at[0],
            device_id=(above, b), device_id_type=MESH,
        )

    def rows_down():
        return pltpu.make_async_remote_copy(
            lowrows.at[pl.ds(3, 3)], low_lo, os_.at[1], or_.at[1],
            device_id=(below, b), device_id_type=MESH,
        )

    def edge_copy(step, side):
        who = (above, m, below)[step + 1]
        return pltpu.make_async_remote_copy(
            opack, oedge.at[1 - step, side], os_.at[2 + 2 * (step + 1) + side],
            or_.at[2 + 2 * (1 - step) + side],
            device_id=(who, (right, left)[side]), device_id_type=MESH,
        )

    def force(low, first):
        rows = len(low)
        low = jnp.concatenate(low, 1)
        open_term = jnp.dot(fl_t[0], low, preferred_element_type=F32)
        ice_term = jnp.dot(fl_t[1], low, preferred_element_type=F32)
        for k in range(rows):
            row = 6 * m - 3 + first + k
            sea = (1 - land[pl.ds(row, 1), :]).astype(F32)
            ice = icem[pl.ds(row, 1), :].astype(F32)
            at = slice(k * W, k * W + W)
            forcing = sea * ((1.0 - ice) * open_term[:, at] + ice * ice_term[:, at])
            mid[first + k] = (oc[row - base].astype(F32) + forcing).astype(BF16)

    has_above = m > 0
    has_below = m < members - 1

    def guarded(flag, act):
        if flag is None:
            act()
        else:
            pl.when(flag)(act)

    guards = {-1: has_above, 0: None, 1: has_below}
    pl.when(has_above)(lambda: rows_up().start())
    pl.when(has_below)(lambda: rows_down().start())
    oc_copy.wait()
    mid[...] = jnp.zeros(mid.shape, BF16)
    mide[...] = jnp.zeros(mide.shape, BF16)
    force([lowrows[k] for k in range(6)], 3)
    edge = pack_edges(lambda k: mid[3 + k], 6)
    fold = turn(edge[0:FOLD], 3)
    for third in range(1, 3):
        fold = jnp.where(
            lanes((FOLD, W)) < 36 * third, fold,
            turn(edge[FOLD * third : FOLD * third + FOLD], 3 + 36 * third),
        )
    opack[...] = fold
    for step in (-1, 1, 0):
        for side in range(2):
            guarded(guards[step], lambda: edge_copy(step, side).start())

    @pl.when(has_below)
    def _():
        rows_up().wait_recv()
        force([low_hi[k] for k in range(3)], 9)

    @pl.when(has_above)
    def _():
        rows_down().wait_recv()
        force([low_lo[k] for k in range(3)], 0)

    def unfold(packed):
        return jnp.concatenate([turn(packed, -3 - 36 * third) for third in range(3)], 0)

    for view, first, count, at in ((0, 0, 6, 3), (-1, 3, 3, 0), (1, 0, 3, 9)):
        def fill(view=view, first=first, count=count, at=at):
            for side in range(2):
                edge_copy(-view, side).wait_recv()
            both = joined_edges(unfold(oedge[view + 1, 0]), unfold(oedge[view + 1, 1]))
            for k in range(count):
                mide[at + k] = turn(both, -SLOT * (first + k))

        guarded(guards[view], fill)

    for g in range(GROUPS):
        out = jnp.dot(bands3[g], conv_part(mid, mide, g, 0), preferred_element_type=F32)
        acc0[0:6, GROUP * g : GROUP * g + GROUP, :] = out.reshape(6, GROUP, W)
    add = branch(acc0, 0, 6, up_t[2], down_t[2], gains[2])
    rows = []
    for k in range(6):
        sea = (1 - land[pl.ds(6 * m + k, 1), :]).astype(F32)
        new = ((mid[3 + k].astype(F32) + scales[2] * add[:, k * W : k * W + W]) * sea).astype(BF16)
        ocean_out[k] = new
        rows.append(new)
    top = jnp.dot(sw_t[...], jnp.concatenate(rows, 1), preferred_element_type=F32).astype(BF16)
    for k in range(6):
        surf[k] = top[:, k * W : k * W + W]

    ocean_store = pltpu.make_async_copy(ocean_out, ocean_hbm_out, out_sem.at[1])
    mine = pl.ds(6 * m, 6)

    def surf_copy(d):
        return pltpu.make_async_remote_copy(
            surf, surfs.at[mine], ss.at[d], sr.at[m], device_id=(d, b), device_id_type=MESH
        )

    def surf_arrival(k):
        return pltpu.make_async_remote_copy(
            surf, surfs.at[pl.ds(6 * k, 6)], ss.at[k], sr.at[k],
            device_id=(k, b), device_id_type=MESH,
        )

    @pl.loop(1, members)
    def _(k):
        surf_copy(lax.rem(m + k, members)).start()

    ocean_store.start()
    surfs[mine] = surf[...]

    @pl.loop(1, members)
    def _(k):
        surf_arrival(lax.rem(m + k, members)).wait_recv()

    surf_store = pltpu.make_async_copy(surfs, surf_hbm, out_sem.at[2])
    surf_store.start()

    pl.when(has_above)(lambda: rows_up().wait_send())
    pl.when(has_below)(lambda: rows_down().wait_send())
    for step in (0, -1, 1):
        for side in range(2):
            guarded(guards[step], lambda: edge_copy(step, side).wait_send())

    @pl.loop(1, members)
    def _(k):
        surf_copy(lax.rem(m + k, members)).wait_send()
        flux_whole(lax.rem(m + k, members)).wait_send()

    y_store.wait()
    ocean_store.wait()
    surf_store.wait()


def couple_kernel(
    y_hbm, o_hbm, surf_hbm, land_hbm, back_hbm, out_hbm, o_out,
    y, o, surf, land, back, y_sem, s_sem, o_sem, out_sem,
):
    n = LAT // CHUNK

    def load(t):
        return pltpu.make_async_copy(
            y_hbm.at[pl.ds(CHUNK * t, CHUNK)], y.at[pl.ds(CHUNK * t, CHUNK)], y_sem.at[t]
        )

    def store(t):
        return pltpu.make_async_copy(
            y.at[pl.ds(CHUNK * t, CHUNK)], out_hbm.at[0, pl.ds(CHUNK * t, CHUNK)], out_sem.at[t]
        )

    small = [
        pltpu.make_async_copy(a, c, s_sem.at[i])
        for i, (a, c) in enumerate(((surf_hbm, surf), (land_hbm, land), (back_hbm, back)))
    ]
    for copy in small:
        copy.start()
    for t in range(n):
        load(t).start()
    o_in = pltpu.make_async_copy(o_hbm, o, o_sem.at[0])
    o_in.start()
    for copy in small:
        copy.wait()
    back_t = jnp.transpose(back[...].astype(F32)).astype(BF16)
    for t in range(n):
        load(t).wait()
        top = jnp.concatenate([surf[CHUNK * t + k] for k in range(CHUNK)], 1)
        add = jnp.dot(back_t, top, preferred_element_type=F32)
        for k in range(CHUNK):
            row = CHUNK * t + k
            sea = (1 - land[row : row + 1, :]).astype(F32)
            y[row] = (y[row].astype(F32) + sea * add[:, k * W : k * W + W]).astype(BF16)
        store(t).start()
    o_in.wait()
    o_back = pltpu.make_async_copy(o, o_out, o_sem.at[1])
    o_back.start()
    for t in range(n):
        store(t).wait()
    o_back.wait()


def local(
    atmos, ocean, land_mask, ice_mask, atm_kernel, atm_gain, atm_up, atm_down, atm_scale,
    flux_weight, flux_lift, ocn_kernel, ocn_gain, ocn_up, ocn_down, ocn_scale,
    surf_weight, back_weight,
):
    hbm = pl.BlockSpec(memory_space=pl.ANY)
    dma = pltpu.SemaphoreType.DMA
    V = pltpu.VMEM
    field = V((ROWS_IN, C, W), BF16)
    packed = V((TILES, C, W), BF16)
    thin = V((3, C, W), BF16)
    small = (
        land_mask, ice_mask, jnp.transpose(atm_kernel, (1, 2, 0, 3)), atm_gain, atm_up,
        jnp.swapaxes(atm_down, 1, 2), atm_scale, flux_weight.T, flux_lift, ocn_kernel,
        ocn_gain.reshape(1, C), ocn_up, ocn_down.T, ocn_scale.reshape(1, C), surf_weight.T,
    )
    y, ocean_rows, surface = pl.pallas_call(
        coupled_kernel,
        out_shape=(
            jax.ShapeDtypeStruct((LAT, C, W), BF16),
            jax.ShapeDtypeStruct((6, C, W), BF16),
            jax.ShapeDtypeStruct((LAT, 8, W), BF16),
        ),
        in_specs=[hbm] * 17,
        out_specs=(hbm, hbm, hbm),
        scratch_shapes=[
            *[V(a.shape, a.dtype) for a in small], V((6, C, W), BF16),
            field, field, field, field, V((TILES * PAIR, C, W), BF16),
            V((GROUPS, GROUP * OUT, DEPTH), BF16), V((GROUPS, GROUP * OUT, DEPTH), BF16),
            V((GROUPS, GROUP * 6, DEPTH), BF16),
            V((PAIR, C, W), F32), V((PAIR, C, W), F32), V((W, W), F32),
            V((3, 384, C), BF16), V((3, C, 384), BF16), V((3, C, W), F32), V((3, C, W), F32),
            V((32, C), BF16), V((2, C, 32), BF16), V((8, C), BF16),
            thin, thin, thin, thin, packed, packed, packed,
            V((TILES * PAIR, 32, W), BF16), V((16, 6, 32, W), BF16),
            V((12, C, W), BF16), V((WIN, C, W), BF16), V((WIN, C, W), BF16), V((FOLD, W), BF16),
            V((3, 2, FOLD, W), BF16),
            V((6, 32, W), BF16), V((3, 32, W), BF16), V((3, 32, W), BF16),
            V((6, 8, W), BF16), V((LAT, 8, W), BF16),
            dma((3,)), dma, dma((3,)), dma((15,)),
            dma((2, 3)), dma((2, 3)), dma((2, TILES)), dma((2, TILES)),
            dma((16,)), dma((16,)), dma((8,)), dma((8,)), dma((16,)), dma((16,)),
        ],
        compiler_params=pltpu.CompilerParams(
            collective_id=0, has_side_effects=True, vmem_limit_bytes=60 * 2**20
        ),
        name="coupled",
    )(atmos, ocean, *small)
    return pl.pallas_call(
        couple_kernel,
        out_shape=(
            jax.ShapeDtypeStruct((1, LAT, C, W), BF16),
            jax.ShapeDtypeStruct((6, C, W), BF16),
        ),
        in_specs=[hbm] * 5,
        out_specs=(hbm, hbm),
        scratch_shapes=[
            V((LAT, C, W), BF16), V((6, C, W), BF16), V((LAT, 8, W), BF16),
            V((LAT, W), jnp.int32), V((8, C), BF16),
            dma((LAT // CHUNK,)), dma((3,)), dma((2,)), dma((LAT // CHUNK,)),
        ],
        compiler_params=pltpu.CompilerParams(vmem_limit_bytes=60 * 2**20),
        name="couple",
    )(y, ocean_rows, surface, land_mask, back_weight)


def solution(mesh):
    in_specs = (
        P("member", None, None, "lon"),
        P(None, None, "lon"),
        P(None, "lon"),
        P(None, "lon"),
    ) + (P(),) * 14
    out_specs = (P("member", None, None, "lon"), P("member", None, "lon"))
    return jax.shard_map(local, mesh=mesh, in_specs=in_specs, out_specs=out_specs, check_vma=False)
```

```python
import jax
import jax.numpy as jnp
from jax import lax
from jax.experimental import pallas as pl
from jax.experimental.pallas import tpu as pltpu
from jax.sharding import PartitionSpec as P

BF16 = jnp.bfloat16
F32 = jnp.float32
MESH = pl.DeviceIdType.MESH

C = 96
W = 128
LAT = 96
GROUP = 16
GROUPS = C // GROUP
OUT = 10
WIN = 16
PAIR = 2 * OUT
TILES = 5
SLOT = 6
FOLD = 32
CHUNK = 32
TAPS = 7
DEPTH = TAPS * WIN * GROUP
ROWS_IN = 106
TANH_A = 2.0 * 0.7978845608028654
TANH_B = 8.0 * 0.7978845608028654 * 0.044715


def half_gelu(half):
    return half + half * jnp.tanh(half * (TANH_A + TANH_B * (half * half)))


def half_gelu_low(half):
    half = half.astype(BF16)
    return half + half * jnp.tanh(half * (BF16(TANH_A) + BF16(TANH_B) * (half * half)))


def lanes(shape):
    return lax.broadcasted_iota(jnp.int32, shape, len(shape) - 1)


def turn(v, shift):
    shift = shift % W
    return v if shift == 0 else pltpu.roll(v, shift, 1)


def band_matrix(kernel_of, taps, bands, outs):
    taps[...] = jnp.zeros(taps.shape, F32)
    for i in range(TAPS):
        taps[8 * i : 8 * i + TAPS, 0:C] = kernel_of(i)
    by_channel = jnp.transpose(taps[...])[0:C].astype(BF16)
    row = lax.broadcasted_iota(jnp.int32, (W, DEPTH), 0)
    lane = lanes((W, DEPTH))
    spread = (row % 8 == lane // (WIN * GROUP)) & (row // 8 == (lane % (WIN * GROUP)) // GROUP)
    wide = jnp.dot(by_channel, spread.astype(F32).astype(BF16), preferred_element_type=F32)
    crow = lax.broadcasted_iota(jnp.int32, (C, DEPTH), 0)
    wide = jnp.where(crow % GROUP == lanes((C, DEPTH)) % GROUP, wide, 0.0).astype(BF16)
    for g in range(GROUPS):
        base = wide[GROUP * g : GROUP * g + GROUP]
        for l in range(outs):
            bands[g, GROUP * l : GROUP * l + GROUP, :] = (
                base if l == 0 else pltpu.roll(base, GROUP * l, 1)
            )


def columns(vector_row):
    return jnp.transpose(jnp.broadcast_to(vector_row, (W, C)))


def shifted(cells, edge, d):
    if d == 0:
        return cells
    lane = lanes(cells.shape)
    if d > 0:
        return pltpu.roll(jnp.where(lane < d, edge, cells), W - d, 1)
    return pltpu.roll(jnp.where(lane >= W + d, edge, cells), -d, 1)


def conv_part(cells, edges, g, row):
    part = cells[pl.ds(row, WIN), GROUP * g : GROUP * g + GROUP, :].reshape(WIN * GROUP, W)
    edge = edges[pl.ds(row, WIN), GROUP * g : GROUP * g + GROUP, :].reshape(WIN * GROUP, W)
    return jnp.concatenate([shifted(part, edge, j - 3) for j in range(TAPS)], 0)


def conv_group(cells, edges, bands, acc, row, g):
    right = jnp.concatenate(
        [conv_part(cells, edges, g, row), conv_part(cells, edges, g, row + OUT)], 1
    )
    out = jnp.dot(bands[g], right, preferred_element_type=F32)
    for half in range(2):
        acc[OUT * half : OUT * half + OUT, GROUP * g : GROUP * g + GROUP, :] = out[
            :, half * W : half * W + W
        ].reshape(OUT, GROUP, W)


def normed(a, gain):
    center = a - jnp.mean(a, axis=0, keepdims=True)
    spread = jnp.mean(center * center, axis=0, keepdims=True)
    return (center * lax.rsqrt(spread + 1e-6) * gain).astype(BF16)


def branch(acc, first, count, up, down, gain):
    n = jnp.concatenate([normed(acc[first + k], gain) for k in range(count)], 1)
    hidden = half_gelu_low(jnp.dot(up, n, preferred_element_type=F32))
    return jnp.dot(down, hidden, preferred_element_type=F32)


def pack_edges(row_of, count):
    lane = lanes((C, W))
    slot = jnp.where(lane >= W - 3, 0, (lane + 3) // SLOT)
    packed = row_of(0)
    for k in range(1, count):
        packed = jnp.where(slot == k, turn(row_of(k), SLOT * k), packed)
    return packed


def pack_thin(row_of, count, shift):
    slot = lanes((C, W)) // 3
    packed = turn(row_of(0), shift)
    for k in range(1, count):
        packed = jnp.where(slot == k, turn(row_of(k), 3 * k + shift), packed)
    return packed


def joined_edges(from_left, from_right):
    lane = lanes((C, W))
    left_side = (lane >= W - 3) | ((lane < W - 5) & ((lane + 3) % SLOT < 3))
    return jnp.where(left_side, from_left, from_right)


def coupled_kernel(
    x_hbm, ocean_hbm, land_h, icem_h, ak_h, ag_h, au_h, ad_h, asc_h, fw_h, fl_h, okn_h, og_h,
    ou_h, od_h, osc_h, sw_h,
    y_hbm, ocean_hbm_out, surf_hbm,
    land, icem, ak, ag, au, ad, asc, fw, fl, okn, og, ou, od, osc, sw, ocean_out,
    xp, xe, yp, ye, y2, bands1, bands2, bands3, acc0, acc1, taps, up_t, down_t, gains, scales,
    fw_t, fl_t, sw_t,
    pack_r, pack_l, fl1, fr1, pack2, fl2, fr2, flux, fluxes, oc, mid, mide, opack,
    oedge, lowrows, low_lo, low_hi, surf,
    in_sem, oc_sem, out_sem, w_sem, s1, r1, s2, r2, fs, fr, os_, or_, ss, sr,
):
    m = lax.axis_index("member")
    b = lax.axis_index("lon")
    members = 16
    bands = 8
    right = lax.rem(b + 1, bands)
    left = lax.rem(b + bands - 1, bands)
    above = lax.rem(m + members - 1, members)
    below = lax.rem(m + 1, members)

    barrier = pltpu.get_barrier_semaphore()
    for side in (left, right):
        for who in (above, m, below):
            pl.semaphore_signal(barrier, inc=1, device_id=(who, side), device_id_type=MESH)

    @pl.loop(1, members)
    def _(k):
        pl.semaphore_signal(
            barrier, inc=1, device_id=(lax.rem(m + k, members), b), device_id_type=MESH
        )

    thin = ((0, 40), (40, 40), (80, 16))

    def load(q):
        first, rows = thin[q]
        return pltpu.make_async_copy(
            x_hbm.at[0, pl.ds(first, rows)], xp.at[pl.ds(3 + first, rows)], in_sem.at[q]
        )

    for q in range(3):
        load(q).start()
    pairs = (
        (ak_h, ak), (au_h, au), (ad_h, ad), (ag_h, ag), (asc_h, asc), (fw_h, fw), (fl_h, fl),
        (okn_h, okn), (og_h, og), (ou_h, ou), (od_h, od), (osc_h, osc), (sw_h, sw),
        (land_h, land), (icem_h, icem),
    )
    small = [pltpu.make_async_copy(a, c, w_sem.at[i]) for i, (a, c) in enumerate(pairs)]
    for copy in small:
        copy.start()
    base = jnp.minimum(jnp.maximum(6 * m - 3, 0), LAT - 12)
    oc_copy = pltpu.make_async_copy(ocean_hbm.at[pl.ds(base, 12)], oc, oc_sem)
    oc_copy.start()

    for ref in (xp, xe, yp, ye):
        ref[0:3] = jnp.zeros((3, C, W), BF16)
        ref[99:ROWS_IN] = jnp.zeros((ROWS_IN - 99, C, W), BF16)

    def thin_sends(q):
        return (
            pltpu.make_async_remote_copy(
                pack_r.at[q], fl1.at[q], s1.at[0, q], r1.at[0, q],
                device_id=(m, right), device_id_type=MESH,
            ),
            pltpu.make_async_remote_copy(
                pack_l.at[q], fr1.at[q], s1.at[1, q], r1.at[1, q],
                device_id=(m, left), device_id_type=MESH,
            ),
        )

    for q in range(3):
        load(q).wait()
        first, rows = thin[q]
        pack_r[q] = pack_thin(lambda k: xp[3 + first + k], rows, 3)
        pack_l[q] = pack_thin(lambda k: xp[3 + first + k], rows, 0)
        if q == 0:
            pl.semaphore_wait(barrier, members - 1 + 6)
        for copy in thin_sends(q):
            copy.start()

    for copy in small:
        copy.wait()
    band_matrix(lambda i: ak[i, :, 0], taps, bands1, OUT)
    for layer in range(2):
        up_t[layer] = (jnp.transpose(au[layer].astype(F32)) * 0.5).astype(BF16)
        down_t[layer] = ad[layer]
        gains[layer] = columns(ag[layer : layer + 1])
        scales[layer] = columns(asc[layer : layer + 1])
    up_t[2] = (jnp.transpose(ou[...].astype(F32)) * 0.5).astype(BF16)
    down_t[2] = od[...]
    gains[2] = columns(og[...])
    scales[2] = columns(osc[...])
    fw_t[...] = fw[...] * BF16(0.5)
    for s in range(2):
        fl_t[s] = jnp.transpose(fl[s].astype(F32)).astype(BF16)
    sw_t[...] = sw[...]
    band_matrix(lambda i: ak[i, :, 1], taps, bands2, OUT)
    band_matrix(lambda i: okn[i], taps, bands3, 6)

    def thin_arrive(q):
        for copy in thin_sends(q):
            copy.wait()

    def thin_spread(p, q, odd):
        lane = lanes((C, W))
        for k in range(min(PAIR, LAT - p * PAIR)):
            at = 3 * (PAIR * odd + k)
            xe[3 + p * PAIR + k] = jnp.where(
                lane < W // 2, turn(fr1[q], -at), turn(fl1[q], -at - 3)
            )

    def sends(p):
        return (
            pltpu.make_async_remote_copy(
                pack2.at[p], fl2.at[p], s2.at[0, p], r2.at[0, p],
                device_id=(m, right), device_id_type=MESH,
            ),
            pltpu.make_async_remote_copy(
                pack2.at[p], fr2.at[p], s2.at[1, p], r2.at[1, p],
                device_id=(m, left), device_id_type=MESH,
            ),
        )

    def arrive(p):
        for copy in sends(p):
            copy.wait()
        both = joined_edges(fl2[p], fr2[p])
        for k in range(PAIR):
            ye[3 + p * PAIR + k] = turn(both, -SLOT * k)

    half = PAIR // 2

    def mlp_one(acc, p, c):
        add = branch(acc, c * half, half, up_t[0], down_t[0], gains[0])
        for k in range(half):
            row = 3 + p * PAIR + c * half + k
            yp[row] = (xp[row].astype(F32) + scales[0] * add[:, k * W : k * W + W]).astype(BF16)

    def mlp_two(acc, p, c):
        add = branch(acc, c * half, half, up_t[1], down_t[1], gains[1])
        rows = []
        for k in range(half):
            row = p * PAIR + c * half + k
            rows.append(
                (yp[3 + row].astype(F32) + scales[1] * add[:, k * W : k * W + W]).astype(BF16)
            )
            y2[row] = rows[k]
        out = half_gelu(
            jnp.dot(fw_t[...], jnp.concatenate(rows, 1), preferred_element_type=F32)
        ).astype(BF16)
        for k in range(half):
            flux[p * PAIR + c * half + k] = out[:, k * W : k * W + W]

    def finish_one(p):
        pack2[p] = pack_edges(lambda k: yp[3 + p * PAIR + k], PAIR)
        for copy in sends(p):
            copy.start()

    def flux_copy(piece):
        d = piece // 3
        return pltpu.make_async_remote_copy(
            flux.at[pl.ds(2 * piece, 2)], fluxes.at[m, pl.ds(2 * lax.rem(piece, 3), 2)],
            fs.at[d], fr.at[m], device_id=(d, b), device_id_type=MESH,
        )

    def flux_whole(k):
        return pltpu.make_async_remote_copy(
            flux.at[pl.ds(6 * k, 6)], fluxes.at[k], fs.at[k], fr.at[k],
            device_id=(k, b), device_id_type=MESH,
        )

    def finish_two(p, first=0, count=half):
        @pl.loop(half * p + first, jnp.minimum(half * p + first + count, 3 * members))
        def _(piece):
            @pl.when(piece // 3 != m)
            def _():
                flux_copy(piece).start()

    def step(mlp, acc, p, conv, next_acc, next_p):
        cells, edges, bands = conv
        for g in range(GROUPS):
            conv_group(cells, edges, bands, next_acc, next_p * PAIR, g)
            if g == 0:
                mlp(acc, p, 0)
            if g == 3:
                mlp(acc, p, 1)

    one = (xp, xe, bands1)
    two = (yp, ye, bands2)
    thin_arrive(0)
    thin_spread(0, 0, 0)
    thin_spread(1, 0, 1)
    for g in range(GROUPS):
        conv_group(*one, acc0, 0, g)

    for p in range(TILES - 1):
        if p % 2 == 0:
            thin_arrive(p // 2 + 1)
        if p + 2 < TILES:
            thin_spread(p + 2, (p + 2) // 2, p % 2)
        acc, next_acc = (acc0, acc1) if p % 2 == 0 else (acc1, acc0)
        step(mlp_one, acc, p, one, next_acc, p + 1)
        finish_one(p)

    kind = lax.rem(m, 3)
    start = (kind + 1) // 2
    stride = 1 - 2 * (kind // 2)

    def order(s):
        return lax.rem(start + stride * s + TILES, TILES)

    for p in range(3):
        arrive(p)
    step(mlp_one, acc0, TILES - 1, two, acc1, start)
    finish_one(TILES - 1)
    yp[99:ROWS_IN] = jnp.zeros((ROWS_IN - 99, C, W), BF16)

    @pl.loop(0, 2)
    def _(t):
        @pl.when(t == 0)
        def _():
            arrive(3)

        step(mlp_two, acc1, order(2 * t), two, acc0, order(2 * t + 1))
        finish_two(order(2 * t))

        @pl.when(t == 0)
        def _():
            arrive(4)
            ye[99:ROWS_IN] = jnp.zeros((ROWS_IN - 99, C, W), BF16)

        step(mlp_two, acc0, order(2 * t + 1), two, acc1, order(2 * t + 2))
        finish_two(order(2 * t + 1))

    for c in range(2):
        mlp_two(acc1, order(4), c)
        finish_two(order(4), c * (half // 2), half // 2)

    y_store = pltpu.make_async_copy(y2.at[pl.ds(0, LAT)], y_hbm, out_sem.at[0])
    y_store.start()

    fluxes[m] = flux[pl.ds(6 * m, 6)]

    @pl.loop(0, members)
    def _(k):
        @pl.when(k != m)
        def _():
            flux_whole(k).wait_recv()

    total = fluxes[0].astype(F32)
    for k in range(1, members):
        total = total + fluxes[k].astype(F32)
    lowrows[...] = (total * (1.0 / members)).astype(BF16)

    def rows_up():
        return pltpu.make_async_remote_copy(
            lowrows.at[pl.ds(0, 3)], low_hi, os_.at[0], or_.at[0],
            device_id=(above, b), device_id_type=MESH,
        )

    def rows_down():
        return pltpu.make_async_remote_copy(
            lowrows.at[pl.ds(3, 3)], low_lo, os_.at[1], or_.at[1],
            device_id=(below, b), device_id_type=MESH,
        )

    def edge_copy(step, side):
        who = (above, m, below)[step + 1]
        return pltpu.make_async_remote_copy(
            opack, oedge.at[1 - step, side], os_.at[2 + 2 * (step + 1) + side],
            or_.at[2 + 2 * (1 - step) + side],
            device_id=(who, (right, left)[side]), device_id_type=MESH,
        )

    def force(low, first):
        rows = len(low)
        low = jnp.concatenate(low, 1)
        open_term = jnp.dot(fl_t[0], low, preferred_element_type=F32)
        ice_term = jnp.dot(fl_t[1], low, preferred_element_type=F32)
        for k in range(rows):
            row = 6 * m - 3 + first + k
            sea = (1 - land[pl.ds(row, 1), :]).astype(F32)
            ice = icem[pl.ds(row, 1), :].astype(F32)
            at = slice(k * W, k * W + W)
            forcing = sea * ((1.0 - ice) * open_term[:, at] + ice * ice_term[:, at])
            mid[first + k] = (oc[row - base].astype(F32) + forcing).astype(BF16)

    has_above = m > 0
    has_below = m < members - 1

    def guarded(flag, act):
        if flag is None:
            act()
        else:
            pl.when(flag)(act)

    guards = {-1: has_above, 0: None, 1: has_below}
    pl.when(has_above)(lambda: rows_up().start())
    pl.when(has_below)(lambda: rows_down().start())
    oc_copy.wait()
    mid[...] = jnp.zeros(mid.shape, BF16)
    mide[...] = jnp.zeros(mide.shape, BF16)
    force([lowrows[k] for k in range(6)], 3)
    edge = pack_edges(lambda k: mid[3 + k], 6)
    fold = turn(edge[0:FOLD], 3)
    for third in range(1, 3):
        fold = jnp.where(
            lanes((FOLD, W)) < 36 * third, fold,
            turn(edge[FOLD * third : FOLD * third + FOLD], 3 + 36 * third),
        )
    opack[...] = fold
    for step in (-1, 1, 0):
        for side in range(2):
            guarded(guards[step], lambda: edge_copy(step, side).start())

    @pl.when(has_below)
    def _():
        rows_up().wait_recv()
        force([low_hi[k] for k in range(3)], 9)

    @pl.when(has_above)
    def _():
        rows_down().wait_recv()
        force([low_lo[k] for k in range(3)], 0)

    def unfold(packed):
        return jnp.concatenate([turn(packed, -3 - 36 * third) for third in range(3)], 0)

    for view, first, count, at in ((0, 0, 6, 3), (-1, 3, 3, 0), (1, 0, 3, 9)):
        def fill(view=view, first=first, count=count, at=at):
            for side in range(2):
                edge_copy(-view, side).wait_recv()
            both = joined_edges(unfold(oedge[view + 1, 0]), unfold(oedge[view + 1, 1]))
            for k in range(count):
                mide[at + k] = turn(both, -SLOT * (first + k))

        guarded(guards[view], fill)

    for g in range(GROUPS):
        out = jnp.dot(bands3[g], conv_part(mid, mide, g, 0), preferred_element_type=F32)
        acc0[0:6, GROUP * g : GROUP * g + GROUP, :] = out.reshape(6, GROUP, W)
    add = branch(acc0, 0, 6, up_t[2], down_t[2], gains[2])
    rows = []
    for k in range(6):
        sea = (1 - land[pl.ds(6 * m + k, 1), :]).astype(F32)
        new = ((mid[3 + k].astype(F32) + scales[2] * add[:, k * W : k * W + W]) * sea).astype(BF16)
        ocean_out[k] = new
        rows.append(new)
    top = jnp.dot(sw_t[...], jnp.concatenate(rows, 1), preferred_element_type=F32).astype(BF16)
    for k in range(6):
        surf[k] = top[:, k * W : k * W + W]

    ocean_store = pltpu.make_async_copy(ocean_out, ocean_hbm_out, out_sem.at[1])
    mine = pl.ds(6 * m, 6)

    def surf_copy(d):
        return pltpu.make_async_remote_copy(
            surf, surf_hbm.at[mine], ss.at[d], sr.at[m], device_id=(d, b), device_id_type=MESH
        )

    def surf_arrival(k):
        return pltpu.make_async_remote_copy(
            surf, surf_hbm.at[pl.ds(6 * k, 6)], ss.at[k], sr.at[k],
            device_id=(k, b), device_id_type=MESH,
        )

    @pl.loop(1, members)
    def _(k):
        surf_copy(lax.rem(m + k, members)).start()

    ocean_store.start()
    surf_store = pltpu.make_async_copy(surf, surf_hbm.at[mine], out_sem.at[2])
    surf_store.start()

    @pl.loop(1, members)
    def _(k):
        surf_arrival(lax.rem(m + k, members)).wait_recv()

    pl.when(has_above)(lambda: rows_up().wait_send())
    pl.when(has_below)(lambda: rows_down().wait_send())
    for step in (0, -1, 1):
        for side in range(2):
            guarded(guards[step], lambda: edge_copy(step, side).wait_send())

    @pl.loop(1, members)
    def _(k):
        surf_copy(lax.rem(m + k, members)).wait_send()
        flux_whole(lax.rem(m + k, members)).wait_send()

    y_store.wait()
    ocean_store.wait()
    surf_store.wait()


def couple_kernel(
    y_hbm, o_hbm, surf_hbm, land_hbm, back_hbm, out_hbm, o_out,
    y, o, surf, land, back, y_sem, s_sem, o_sem, out_sem,
):
    n = LAT // CHUNK

    def load(t):
        return pltpu.make_async_copy(
            y_hbm.at[pl.ds(CHUNK * t, CHUNK)], y.at[pl.ds(CHUNK * t, CHUNK)], y_sem.at[t]
        )

    def store(t):
        return pltpu.make_async_copy(
            y.at[pl.ds(CHUNK * t, CHUNK)], out_hbm.at[0, pl.ds(CHUNK * t, CHUNK)], out_sem.at[t]
        )

    small = [
        pltpu.make_async_copy(a, c, s_sem.at[i])
        for i, (a, c) in enumerate(((surf_hbm, surf), (land_hbm, land), (back_hbm, back)))
    ]
    for copy in small:
        copy.start()
    for t in range(n):
        load(t).start()
    o_in = pltpu.make_async_copy(o_hbm, o, o_sem.at[0])
    o_in.start()
    for copy in small:
        copy.wait()
    back_t = jnp.transpose(back[...].astype(F32)).astype(BF16)
    for t in range(n):
        load(t).wait()
        top = jnp.concatenate([surf[CHUNK * t + k] for k in range(CHUNK)], 1)
        add = jnp.dot(back_t, top, preferred_element_type=F32)
        for k in range(CHUNK):
            row = CHUNK * t + k
            sea = (1 - land[row : row + 1, :]).astype(F32)
            y[row] = (y[row].astype(F32) + sea * add[:, k * W : k * W + W]).astype(BF16)
        store(t).start()
    o_in.wait()
    o_back = pltpu.make_async_copy(o, o_out, o_sem.at[1])
    o_back.start()
    for t in range(n):
        store(t).wait()
    o_back.wait()


def local(
    atmos, ocean, land_mask, ice_mask, atm_kernel, atm_gain, atm_up, atm_down, atm_scale,
    flux_weight, flux_lift, ocn_kernel, ocn_gain, ocn_up, ocn_down, ocn_scale,
    surf_weight, back_weight,
):
    hbm = pl.BlockSpec(memory_space=pl.ANY)
    dma = pltpu.SemaphoreType.DMA
    V = pltpu.VMEM
    field = V((ROWS_IN, C, W), BF16)
    packed = V((TILES, C, W), BF16)
    thin = V((3, C, W), BF16)
    small = (
        land_mask, ice_mask, jnp.transpose(atm_kernel, (1, 2, 0, 3)), atm_gain, atm_up,
        jnp.swapaxes(atm_down, 1, 2), atm_scale, flux_weight.T, flux_lift, ocn_kernel,
        ocn_gain.reshape(1, C), ocn_up, ocn_down.T, ocn_scale.reshape(1, C), surf_weight.T,
    )
    y, ocean_rows, surface = pl.pallas_call(
        coupled_kernel,
        out_shape=(
            jax.ShapeDtypeStruct((LAT, C, W), BF16),
            jax.ShapeDtypeStruct((6, C, W), BF16),
            jax.ShapeDtypeStruct((LAT, 8, W), BF16),
        ),
        in_specs=[hbm] * 17,
        out_specs=(hbm, hbm, hbm),
        scratch_shapes=[
            *[V(a.shape, a.dtype) for a in small], V((6, C, W), BF16),
            field, field, field, field, V((TILES * PAIR, C, W), BF16),
            V((GROUPS, GROUP * OUT, DEPTH), BF16), V((GROUPS, GROUP * OUT, DEPTH), BF16),
            V((GROUPS, GROUP * 6, DEPTH), BF16),
            V((PAIR, C, W), F32), V((PAIR, C, W), F32), V((W, W), F32),
            V((3, 384, C), BF16), V((3, C, 384), BF16), V((3, C, W), F32), V((3, C, W), F32),
            V((32, C), BF16), V((2, C, 32), BF16), V((8, C), BF16),
            thin, thin, thin, thin, packed, packed, packed,
            V((TILES * PAIR, 32, W), BF16), V((16, 6, 32, W), BF16),
            V((12, C, W), BF16), V((WIN, C, W), BF16), V((WIN, C, W), BF16), V((FOLD, W), BF16),
            V((3, 2, FOLD, W), BF16),
            V((6, 32, W), BF16), V((3, 32, W), BF16), V((3, 32, W), BF16),
            V((6, 8, W), BF16),
            dma((3,)), dma, dma((3,)), dma((15,)),
            dma((2, 3)), dma((2, 3)), dma((2, TILES)), dma((2, TILES)),
            dma((16,)), dma((16,)), dma((8,)), dma((8,)), dma((16,)), dma((16,)),
        ],
        compiler_params=pltpu.CompilerParams(
            collective_id=0, has_side_effects=True, vmem_limit_bytes=60 * 2**20
        ),
        name="coupled",
    )(atmos, ocean, *small)
    return pl.pallas_call(
        couple_kernel,
        out_shape=(
            jax.ShapeDtypeStruct((1, LAT, C, W), BF16),
            jax.ShapeDtypeStruct((6, C, W), BF16),
        ),
        in_specs=[hbm] * 5,
        out_specs=(hbm, hbm),
        scratch_shapes=[
            V((LAT, C, W), BF16), V((6, C, W), BF16), V((LAT, 8, W), BF16),
            V((LAT, W), jnp.int32), V((8, C), BF16),
            dma((LAT // CHUNK,)), dma((3,)), dma((2,)), dma((LAT // CHUNK,)),
        ],
        compiler_params=pltpu.CompilerParams(vmem_limit_bytes=60 * 2**20),
        name="couple",
    )(y, ocean_rows, surface, land_mask, back_weight)


def solution(mesh):
    in_specs = (
        P("member", None, None, "lon"),
        P(None, None, "lon"),
        P(None, "lon"),
        P(None, "lon"),
    ) + (P(),) * 14
    out_specs = (P("member", None, None, "lon"), P("member", None, "lon"))
    return jax.shard_map(local, mesh=mesh, in_specs=in_specs, out_specs=out_specs, check_vma=False)
```
